32 devices in a mesh: slab: 2 (over x), sx: 4 (over y, core), sy: 4 (over z).
Axes of the slice: x: 2, y: 2, z: 4, core: 2. Of those that a mesh axis runs over, the one named last changes fastest.
Arguments:
- start_states: float32 [2, 512, 1024], P('slab', 'sx', 'sy'), may hold values from -6 to 6
- source: float32 [2, 512, 1024], P('slab', 'sx', 'sy'), may hold values from -5 to 5
- cond_field: float32 [512, 1024], P('sx', 'sy'), may hold values from 0.5 to 2
- materials: int32 [64, 128], P('sx', 'sy'), may hold values from 0 to 1
- conductivity: float32 [2], replicated, may hold values from 1 to 4
- sink_rate: float32 [2], replicated, may hold values from 0.5 to 3
Outputs:
- defect: float32 [2, 512, 1024], P('slab', 'sx', 'sy')
- gradient: float32 [2, 512, 1024], P('slab', 'sx', 'sy')
The draws below stay inside these ranges and needn't reach their ends.
Inputs may be any that keep to these rules, and one draw needn't show every extreme that they name: `materials`: 0 marks mold, 1 marks gob.
All inputs are finite; a program needn't handle non-finite values.
Results may differ from the reference program's by a relative error of at most 0.0001.
Values sent between devices are 32-bit elements; how exact they have to be, the bound alone decides.
No kernel may reach another device: no remote copies, remote signals or barrier semaphores. Data moves between devices by JAX's collectives and lax.ppermute only.
A program may use at most 64 MiB of HBM per device.

```python
import math
import jax
import jax.numpy as jnp
from jax import lax

BLOCK = 8
STEPS = 3
NEWTON = 2
JACOBI = 4
SLABS = 2
NX = 512
NY = 1024


def draw_source(key, part):
    return jnp.clip(jax.random.normal(key, (SLABS, NX, NY), jnp.float32), -5.0, 5.0)


def set_ends(array, own_key, smallest, high):
    longest = array.shape.index(max(array.shape))
    spots = []
    for shift in (0, 1):
        where = [jax.random.randint(jax.random.fold_in(own_key, axis), (), 0, length) for axis, length in enumerate(array.shape)]
        where[longest] = (where[longest] + shift) % array.shape[longest]
        spots.append(tuple(where))
    return array.at[spots[0]].set(smallest).at[spots[1]].set(high)


def level_of(stream_key, extent, cuts, low, largest):
    gain, own = 1.0, jax.random.fold_in(stream_key, 6)
    for dim, shards_of in cuts:
        draws = jnp.exp(jax.random.uniform(jax.random.fold_in(own, dim), (shards_of,), jnp.float32, low / len(cuts), largest / len(cuts)))
        gain = gain * jnp.repeat(draws, extent[dim] // shards_of).reshape([-1 if axis == dim else 1 for axis in range(len(extent))])
    return gain


def scatter_about(key, shape, spread, most, shards=(), kind=jnp.bfloat16):
    values = spread * jax.random.normal(key, shape, jnp.float32)
    if shards:
        values = values * level_of(key, shape, shards, -0.22, 0.18)
    return jnp.clip(values, -most, most).astype(kind)


def setup_inputs(seed: int = 0) -> dict:
    key_list = jax.random.split(jax.random.key(seed), 7)
    start_states = scatter_about(key_list[0], (SLABS, NX, NY), 1.0, 6.0, ((0, 2), (1, 4), (2, 4)), jnp.float32)
    source = draw_source(jax.random.fold_in(key_list[6], 71), 0)
    cond_field = jnp.clip(jnp.exp(math.log(2.0) - 1.3862944 * jax.random.uniform(key_list[2], (NX, NY), jnp.float32) ** level_of(key_list[2], (NX, NY), ((0, 4), (1, 4)), -0.2, 0.2)), 0.5, 2.0)
    materials = set_ends(jax.random.randint(key_list[3], (NX // BLOCK, NY // BLOCK), 0, 2), jax.random.fold_in(key_list[3], 1), 0, 1).astype(jnp.int32)
    conductivity = jnp.clip(jnp.exp(jax.random.uniform(key_list[4], (2,), jnp.float32, math.log(1.0), math.log(4.0))), 1.0, 4.0)
    sink_rate = jnp.clip(jnp.exp(jax.random.uniform(key_list[5], (2,), jnp.float32, math.log(0.5), math.log(3.0))), 0.5, 3.0)
    return dict(start_states=start_states, source=source, cond_field=cond_field, materials=materials, conductivity=conductivity, sink_rate=sink_rate)


time_step = 2.0


def edge_terms(kappa_padded):
    center = kappa_padded[1:-1, 1:-1]
    west_edge = 0.5 * (center + kappa_padded[:-2, 1:-1])
    east_edge = 0.5 * (center + kappa_padded[2:, 1:-1])
    south_edge = 0.5 * (center + kappa_padded[1:-1, :-2])
    north_edge = 0.5 * (center + kappa_padded[1:-1, 2:])
    return west_edge, east_edge, south_edge, north_edge


def factor(diagonal, east_edge):
    blocks = diagonal.shape[0] // BLOCK
    pivots_in = diagonal.reshape(blocks, BLOCK, diagonal.shape[1])
    upper = (-time_step * east_edge).reshape(blocks, BLOCK, diagonal.shape[1])
    inverse = [1.0 / pivots_in[:, 0]]
    ratios = [upper[:, 0] * inverse[0]]
    for position in range(1, BLOCK):
        pivot = pivots_in[:, position] - upper[:, position - 1] * ratios[position - 1]
        inverse.append(1.0 / pivot)
        if position < BLOCK - 1:
            ratios.append(upper[:, position] * inverse[position])
    return upper, ratios, inverse


def block_solve(factors, right):
    upper, ratios, inverse = factors
    blocks = right.shape[0] // BLOCK
    shaped = right.reshape(blocks, BLOCK, right.shape[1])
    forward_vals = [shaped[:, 0] * inverse[0]]
    for position in range(1, BLOCK):
        forward_vals.append((shaped[:, position] - upper[:, position - 1] * forward_vals[position - 1]) * inverse[position])
    result = list(forward_vals)
    for position in range(BLOCK - 2, -1, -1):
        result[position] = forward_vals[position] - ratios[position] * result[position + 1]
    return jnp.stack(result, axis=1).reshape(right.shape)


def jacobi(factors, edges, first_row, last_row, right, pad_fn):
    west_edge, east_edge, south_edge, north_edge = edges
    answer = block_solve(factors, right)
    for counter in range(JACOBI - 1):
        padded = pad_fn(answer)
        coupled = (first_row * west_edge * padded[:-2, 1:-1] + last_row * east_edge * padded[2:, 1:-1]
                   + south_edge * padded[1:-1, :-2] + north_edge * padded[1:-1, 2:])
        answer = block_solve(factors, right + time_step * coupled)
    return answer


def implicit_step(previous, forcing, sink_node, edges, first_row, last_row, state_pad, sweep_pad):
    west_edge, east_edge, south_edge, north_edge = edges
    edge_sum = west_edge + east_edge + south_edge + north_edge
    current = previous
    for newton_it in range(NEWTON):
        padded = state_pad(current)
        laplace = (edge_sum * current - west_edge * padded[:-2, 1:-1] - east_edge * padded[2:, 1:-1]
                   - south_edge * padded[1:-1, :-2] - north_edge * padded[1:-1, 2:])
        tangent = jnp.tanh(current)
        diagonal = 1.0 + time_step * (edge_sum + sink_node * (1.0 - tangent * tangent))
        residual = previous - current - time_step * (laplace + sink_node * tangent - forcing)
        factors = factor(diagonal, east_edge)
        current = current + jacobi(factors, edges, first_row, last_row, residual, sweep_pad)
    return current


def adjoint_step(state, weight, sink_node, edges, first_row, last_row, sweep_pad):
    west_edge, east_edge, south_edge, north_edge = edges
    edge_sum = west_edge + east_edge + south_edge + north_edge
    tangent = jnp.tanh(state)
    diagonal = 1.0 + time_step * (edge_sum + sink_node * (1.0 - tangent * tangent))
    return jacobi(factor(diagonal, east_edge), edges, first_row, last_row, weight, sweep_pad)


def padder(field):
    return jnp.pad(field, 1)


def reference(start_states, source, cond_field, materials, conductivity, sink_rate):
    node_material = jnp.repeat(jnp.repeat(materials, BLOCK, axis=0), BLOCK, axis=1)
    kappa_node = jnp.where(node_material == 1, conductivity[1], conductivity[0]) * cond_field
    sink_node = jnp.where(node_material == 1, sink_rate[1], sink_rate[0])
    edges = edge_terms(jnp.pad(kappa_node, 1))
    row_ids = jnp.arange(NX) % BLOCK
    first_row = jnp.where(row_ids == 0, 1.0, 0.0).astype(jnp.float32)[:, None]
    last_row = jnp.where(row_ids == BLOCK - 1, 1.0, 0.0).astype(jnp.float32)[:, None]

    def advance(slab_inputs):
        current, forcing = slab_inputs
        states = []
        for step_no in range(STEPS):
            current = implicit_step(current, forcing, sink_node, edges, first_row, last_row, padder, padder)
            states.append(current)
        return jnp.stack(states)

    states = lax.map(advance, (start_states, source))
    defect = jnp.roll(states[:, STEPS - 1], 1, axis=0) - start_states
    following = jnp.roll(defect, -1, axis=0)

    def retreat(slab_inputs):
        saved_states, weight = slab_inputs
        for step_no in range(STEPS - 1, -1, -1):
            weight = adjoint_step(saved_states[step_no], weight, sink_node, edges, first_row, last_row, padder)
        return weight

    carried = lax.map(retreat, (states, following))
    return defect, carried - defect
```

```python
import functools

import jax
import jax.numpy as jnp
from jax import lax
from jax.experimental import pallas as pl
from jax.experimental.pallas import tpu as pltpu
from jax.sharding import PartitionSpec as P

BLOCK = 8
STEPS = 3
NEWTON = 2
JACOBI = 4
LANES = 128
HALO = 32
STRIP = LANES - 2 * HALO
CHUNK = 16

time_step = 2.0
half_step = 0.5 * time_step

VMEM = pl.BlockSpec(memory_space=pltpu.VMEM)
SMEM = pl.BlockSpec(memory_space=pltpu.SMEM)
F32 = jnp.float32


def roll(x, shift):
    return pltpu.roll(x, shift % LANES, axis=x.ndim - 1)


def lanes_of(x):
    return lax.broadcasted_iota(jnp.int32, x.shape, x.ndim - 1)


def pick(test, a, b):
    return jnp.where(test, a, b)


TILE = 3 * BLOCK + 1
HALF = BLOCK + 1
WIDE = 4 * BLOCK + 1


def first_pack(s, f, k):
    at = lanes_of(s)
    far = jnp.where(at == 96, roll(s, 64), roll(k, 65))
    return jnp.where(at < 32, s, jnp.where(at < 64, roll(f, 32), jnp.where(at < 96, roll(k, 64), far)))


def last_pack(s, f, k):
    at = lanes_of(s)
    far = jnp.where(at == 96, roll(s, 1), roll(k, 2))
    return jnp.where(at < 32, roll(s, 32), jnp.where(at < 64, roll(f, 64), jnp.where(at < 96, roll(k, 96), far)))


def pack_kernel(pos, conductivity, start, source, cond, materials, own, flip, along, across, split):
    y = pos[0]
    count, cells = materials.shape
    width = start.shape[1]
    column = lax.broadcasted_iota(jnp.int32, (cells, width), 1)
    cell = lax.broadcasted_iota(jnp.int32, (cells, width), 0)
    spread = jnp.where(column // BLOCK == cell, 1.0, 0.0).astype(F32)
    material = jnp.dot(materials[...].astype(F32), spread, preferred_element_type=F32)
    is_gob = material > 0.5
    factor = jnp.where(is_gob, conductivity[1], conductivity[0])
    m0, m1 = material[:, :LANES], material[:, LANES:]
    lower = y == 0

    def place(p, tiles, packs):
        (first0, last0, first1, last1) = packs
        if tiles is not None:
            for a, (x0, x1) in enumerate(tiles):
                own[a * BLOCK + p] = pick(lower, x0, x1)
                flip[a * BLOCK + p] = pick(lower, x1, x0)
        own[TILE + p] = pick(lower, first1, last0)
        flip[TILE + p] = pick(lower, last0, first1)
        along[p] = pick(lower, last1, first0)
        across[p] = pick(lower, first0, last1)

    for a, ref in enumerate((start, source, cond)):
        split[2 * a] = ref[:, :LANES]
        split[2 * a + 1] = ref[:, LANES:]
    for p in range(BLOCK):
        rows = pl.ds(p, count, stride=BLOCK)
        s0, s1, f0, f1, k0, k1 = (split[a, rows, :] for a in range(6))
        k0, k1 = k0 * factor[:, :LANES], k1 * factor[:, LANES:]
        packs = (first_pack(s0, f0, k0), last_pack(s0, f0, k0), first_pack(s1, f1, k1), last_pack(s1, f1, k1))
        place(p, ((s0, s1), (f0, f1), (k0, k1)), packs)
    own[3 * BLOCK] = pick(lower, m0, m1)
    flip[3 * BLOCK] = pick(lower, m1, m0)
    place(BLOCK, None, (m0, roll(m0, 32), m1, roll(m1, 32)))


def window_kernel(pos, own, other, along, across, mine, theirs):
    lower = pos[0] == 0
    even = pos[1] == 0
    at = lax.broadcasted_iota(jnp.int32, own.shape[1:], 1)

    def put(slot, index, left, right):
        mine[slot, index] = pick(even, left, right)
        theirs[slot, index] = pick(even, right, left)

    for slot, (tile, outer) in enumerate(((own, along), (other, across))):
        for p in range(BLOCK + 1):
            inner, far = tile[TILE + p], outer[p]
            west, east = pick(lower, far, inner), pick(lower, inner, far)
            if p == BLOCK:
                m = tile[3 * BLOCK]
                put(slot, 4 * BLOCK, jnp.where(at < 32, west, roll(m, 32)), jnp.where(at >= 96, roll(east, 96), roll(m, 96)))
                continue
            s, f, k = tile[p], tile[BLOCK + p], tile[2 * BLOCK + p]
            for a, x in enumerate((s, f, k)):
                left = jnp.where(at < 32, roll(west, -32 * a), roll(x, 32))
                right = jnp.where(at >= 96, roll(east, 96 - 32 * a), roll(x, 96))
                put(slot, a * BLOCK + p, left, right)
            left = jnp.where(at < 2, roll(west, 32), jnp.where(at == 127, roll(s, 31), roll(k, 30)))
            right = jnp.where(at == 0, roll(s, 97), jnp.where(at == 1, roll(k, 98), jnp.where(at == 127, roll(east, 31), roll(east, 29))))
            put(slot, 3 * BLOCK + p, left, right)


def chunks(lines):
    for first in range(0, lines, CHUNK):
        yield first


def shifted(ref, p, first, by):
    return ref[p, pl.ds(BLOCK + first + by, CHUNK), :]


def padded(ref, p, first):
    return ref[p, pl.ds(BLOCK + first, CHUNK), :]


def put_padded(ref, p, first, value):
    ref[p, pl.ds(BLOCK + first, CHUNK), :] = value


def clear_ends(ref, lines):
    zero = jnp.zeros((BLOCK, LANES), F32)
    for p in (0, BLOCK - 1):
        ref[p, 0:BLOCK, :] = zero
        ref[p, BLOCK + lines : 2 * BLOCK + lines, :] = zero


def factor_and_solve(first, diagonal, right, south, north, east, west, scaled, answer):
    at = pl.ds(first, CHUNK)
    keep_right, keep_south, keep_north, keep_lower, keep_upper, keep_ends = scaled
    values = []
    ratio = None
    value = None
    edge = None
    for p in range(BLOCK):
        pivot = diagonal(p)
        if p:
            pivot = pivot - edge * ratio
        inverse = 1.0 / pivot
        scaled_right = right(p) * inverse
        keep_right[p, at, :] = scaled_right
        keep_south[p, at, :] = south[p, at, :] * inverse
        keep_north[p, at, :] = north[p, at, :] * inverse
        if p == 0:
            keep_ends[0, at, :] = west[at, :] * inverse
            value = scaled_right
        else:
            lower = edge * inverse
            keep_lower[p, at, :] = lower
            value = scaled_right + lower * value
        edge = east[p, at, :]
        ratio = edge * inverse
        if p < BLOCK - 1:
            keep_upper[p, at, :] = ratio
        else:
            keep_ends[1, at, :] = ratio
        values.append(value)
    back_substitute(first, values, keep_upper, lambda p, z: put_padded(answer, p, first, z))


def back_substitute(first, values, upper, store):
    at = pl.ds(first, CHUNK)
    z = values[BLOCK - 1]
    store(BLOCK - 1, z)
    for p in range(BLOCK - 2, -1, -1):
        z = values[p] + upper[p, at, :] * z
        store(p, z)


def sweep(lines, scaled, old, store):
    keep_right, keep_south, keep_north, keep_lower, keep_upper, keep_ends = scaled
    for first in chunks(lines):
        at = pl.ds(first, CHUNK)
        values = []
        for p in range(BLOCK):
            z = padded(old, p, first)
            value = keep_right[p, at, :] + keep_south[p, at, :] * roll(z, 1) + keep_north[p, at, :] * roll(z, -1)
            if p == 0:
                value = value + keep_ends[0, at, :] * shifted(old, BLOCK - 1, first, -1)
            if p == BLOCK - 1:
                value = value + keep_ends[1, at, :] * shifted(old, 0, first, 1)
            if p:
                value = value + keep_lower[p, at, :] * values[-1]
            values.append(value)
        back_substitute(first, values, keep_upper, functools.partial(store, first))


def put_into(ref):
    return lambda first, p, z: put_padded(ref, p, first, z)


def forward_kernel(pos, sinks, mine, theirs, states, south, north, east, west, base, sink, level, forcing, kappa, edge, previous, old, new, *scaled):
    y, c, strip, strips = pos[0], pos[1], pos[2], pos[3]
    lines = base.shape[1]
    count = mine.shape[2]
    for ref in (level, kappa, old, new):
        clear_ends(ref, lines)
    lane = lax.broadcasted_iota(jnp.int32, (count, LANES), 1)
    column = strip * STRIP - HALO + lane
    inside = (column >= 0) & (column < strips * STRIP)

    for ref, core in ((mine, c), (theirs, 1 - c)):
        for slot in range(2):
            chip = y if slot == 0 else 1 - y
            first = pl.multiple_of((2 * chip + core) * count, BLOCK)
            for p in range(BLOCK):
                level[p, pl.ds(BLOCK + first, count), :] = ref[slot, p]
                forcing[p, pl.ds(first, count), :] = time_step * ref[slot, BLOCK + p]
                kappa[p, pl.ds(BLOCK + first, count), :] = jnp.where(inside, ref[slot, 2 * BLOCK + p], 0.0)
                edge[p, pl.ds(first, count), :] = ref[slot, 3 * BLOCK + p]
            sink[pl.ds(first, count), :] = time_step * jnp.where(ref[slot, 4 * BLOCK] > 0.5, sinks[1], sinks[0])

    lane = lax.broadcasted_iota(jnp.int32, (CHUNK, LANES), 1)
    column = strip * STRIP - HALO + lane
    is_first = lane == 0
    is_last = lane == LANES - 1
    has_south = column != 0
    has_north = column != strips * STRIP - 1
    before = strip * STRIP - HALO > 0
    after = strip * STRIP - HALO + LANES < strips * STRIP

    for first in chunks(lines):
        at = pl.ds(first, CHUNK)
        k = [padded(kappa, p, first) for p in range(BLOCK)]
        wests = [half_step * (k[0] + shifted(kappa, BLOCK - 1, first, -1))]
        wests += [half_step * (k[p] + k[p - 1]) for p in range(1, BLOCK)]
        wests += [half_step * (k[BLOCK - 1] + shifted(kappa, 0, first, 1))]
        west[at, :] = wests[0]
        for p in range(BLOCK):
            side = edge[p, at, :]
            below = jnp.where(is_first, jnp.where(before, roll(side, -1), 0.0), roll(k[p], 1))
            above = jnp.where(is_last, jnp.where(after, roll(side, 1), 0.0), roll(k[p], -1))
            s = half_step * (k[p] + below)
            n = half_step * (k[p] + above)
            base[p, at, :] = 1.0 + (wests[p] + wests[p + 1] + s + n)
            south[p, at, :] = jnp.where(has_south, s, 0.0)
            north[p, at, :] = jnp.where(has_north, n, 0.0)
            east[p, at, :] = wests[p + 1]

    def newton(from_previous):
        for first in chunks(lines):
            at = pl.ds(first, CHUNK)
            sink_here = sink[at, :]
            tangents = {}
            currents = {}

            def state(p):
                if p not in currents:
                    currents[p] = padded(level, p, first)
                    tangents[p] = jnp.tanh(currents[p])
                return currents[p], tangents[p]

            def diagonal(p):
                _, tangent = state(p)
                return base[p, at, :] + sink_here * (1.0 - tangent * tangent)

            def right(p):
                current, tangent = state(p)
                side = edge[p, at, :]
                below = jnp.where(is_first, side, roll(current, 1))
                above = jnp.where(is_last, side, roll(current, -1))
                behind = padded(level, p - 1, first) if p else shifted(level, BLOCK - 1, first, -1)
                ahead = padded(level, p + 1, first) if p < BLOCK - 1 else shifted(level, 0, first, 1)
                behind_edge = east[p - 1, at, :] if p else west[at, :]
                pulled = (south[p, at, :] * below + north[p, at, :] * above + behind_edge * behind + east[p, at, :] * ahead)
                if from_previous:
                    held = (1.0 - base[p, at, :]) * current
                else:
                    held = previous[p, at, :] - base[p, at, :] * current
                return held + pulled - sink_here * tangent + forcing[p, at, :]

            factor_and_solve(first, diagonal, right, south, north, east, west, scaled, old)
        sweep(lines, scaled, old, put_into(new))
        sweep(lines, scaled, new, put_into(old))
        sweep(lines, scaled, old, lambda first, p, z: put_padded(level, p, first, padded(level, p, first) + z))

    def step(number, carry):
        for p in range(BLOCK):
            previous[p] = level[p, pl.ds(BLOCK, lines), :]
        newton(True)
        for _ in range(1, NEWTON):
            newton(False)
        for p in range(BLOCK):
            states[number * BLOCK + p] = level[p, pl.ds(BLOCK, lines), :]
        return carry

    lax.fori_loop(0, STEPS, step, 0)


def adjoint_kernel(states, weight, south, north, east, west, base, sink, out, old, new, given, *scaled):
    lines = base.shape[1]
    for ref in (old, new):
        clear_ends(ref, lines)
    for p in range(BLOCK):
        given[p] = weight[p]

    def step(number, carry):
        level = STEPS - 1 - number
        for first in chunks(lines):
            at = pl.ds(first, CHUNK)
            sink_here = sink[at, :]

            def diagonal(p):
                tangent = jnp.tanh(states[level * BLOCK + p, at, :])
                return base[p, at, :] + sink_here * (1.0 - tangent * tangent)

            def right(p):
                return given[p, at, :]

            factor_and_solve(first, diagonal, right, south, north, east, west, scaled, old)
        sweep(lines, scaled, old, put_into(new))
        sweep(lines, scaled, new, put_into(old))

        def store(first, p, z):
            given[p, pl.ds(first, CHUNK), :] = z

        sweep(lines, scaled, old, store)
        return carry

    lax.fori_loop(0, STEPS, step, 0)
    count = out.shape[2]
    at = lax.broadcasted_iota(jnp.int32, (count, LANES), 1)
    for core in range(2):
        for p in range(BLOCK):
            low = given[p, pl.ds(core * count, count), :]
            high = given[p, pl.ds((2 + core) * count, count), :]
            out[core, p] = jnp.where(at < STRIP, roll(low, -HALO), roll(high, HALO))


def defect_kernel(pos, states, mine, theirs, weight, out):
    y, c = pos[0], pos[1]
    count = mine.shape[2]
    at = lax.broadcasted_iota(jnp.int32, (count, LANES), 1)
    for ref, core in ((mine, c), (theirs, 1 - c)):
        for p in range(BLOCK):
            ends = []
            for slot in range(2):
                chip = y if slot == 0 else 1 - y
                first = pl.multiple_of((2 * chip + core) * count, BLOCK)
                value = states[(STEPS - 1) * BLOCK + p, pl.ds(first, count), :] - ref[slot, p]
                weight[p, pl.ds(first, count), :] = value
                ends.append(value)
            low, high = pick(y == 0, ends[0], ends[1]), pick(y == 0, ends[1], ends[0])
            out[core, p] = jnp.where(at < STRIP, roll(low, -HALO), roll(high, HALO))


def swap_kernel(pos, adjoint, defect, keep, send):
    c = pos[1]
    for p in range(BLOCK):
        for a in range(2):
            other = defect[1 - c, p]
            held = defect[c, p]
            if a == 0:
                other = adjoint[1 - c, p] - other
                held = adjoint[c, p] - held
            keep[a, p] = held
            send[a, p] = other


def tile_kernel(pos, mine, theirs, keep, send):
    y, c = pos[0], pos[1]
    count = mine.shape[2]
    at = lax.broadcasted_iota(jnp.int32, (count, LANES), 1)
    for a in range(2):
        for p in range(BLOCK):
            even = pick(c == 0, mine[a, p], theirs[a, p])
            odd = pick(c == 0, theirs[a, p], mine[a, p])
            chip0 = jnp.where(at < STRIP, even, roll(odd, STRIP))
            chip1 = jnp.where(at < STRIP, roll(even, STRIP), odd)
            rows = pl.ds(p, count, stride=BLOCK)
            keep[a, rows, :] = pick(y == 0, chip0, chip1)
            send[a, rows, :] = pick(y == 0, chip1, chip0)


def join_kernel(pos, mine, theirs, gradient, defect):
    lower = pos[0] == 0
    for a, ref in enumerate((gradient, defect)):
        ref[:, :LANES] = pick(lower, mine[a], theirs[a])
        ref[:, LANES:] = pick(lower, theirs[a], mine[a])


def per_device(slabs, strips_y, start_states, source, cond_field, materials, conductivity, sink_rate):
    sx = lax.axis_index("sx")
    z = lax.axis_index("sy")
    y, c = sx // 2, sx % 2
    pos = jnp.stack([y, c, 4 * z + sx, jnp.int32(4 * strips_y)]).astype(jnp.int32)
    start, forcing = start_states[0], source[0]
    rows = start.shape[0]
    count = rows // BLOCK
    lines = 4 * count
    shape = lambda *dims: jax.ShapeDtypeStruct(dims, F32)
    params = pltpu.CompilerParams(vmem_limit_bytes=48 * 1024 * 1024)

    def call(body, outs, ins, scratch=(), flops=0):
        specs = [SMEM if s else VMEM for s in ins]
        cost = pl.CostEstimate(flops=flops, bytes_accessed=1 << 20, transcendentals=0)
        return pl.pallas_call(body, out_shape=outs, in_specs=specs, out_specs=[VMEM] * len(outs), scratch_shapes=list(scratch), compiler_params=params, cost_estimate=cost)

    def joint(y_, c_, z_):
        return (2 * y_ + c_) * strips_y + z_

    everyone = [(a, b, d) for a in range(2) for b in range(2) for d in range(strips_y)]
    top = strips_y - 1

    def along_to(a, b, d):
        if a == 1:
            return (1, b, d - 1) if d > 0 else (0, b, d)
        return (0, b, d + 1) if d < top else (1, b, d)

    def across_to(a, b, d):
        if a == 1:
            return (0, b, d + 1) if d < top else (1, b, d)
        return (1, b, d - 1) if d > 0 else (0, b, d)

    along_pairs = [(joint(*v), joint(*along_to(*v))) for v in everyone]
    across_pairs = [(joint(*v), joint(*across_to(*v))) for v in everyone]
    flip_pairs = [(0, 2), (1, 3), (2, 0), (3, 1)]
    core_pairs = [(0, 1), (1, 0), (2, 3), (3, 2)]
    forth = [(i, (i + 1) % slabs) for i in range(slabs)]
    back = [(b, a) for a, b in forth]

    own, flip, along, across = call(
        pack_kernel,
        [shape(TILE + HALF, count, LANES)] * 2 + [shape(HALF, count, LANES)] * 2,
        (1, 1, 0, 0, 0, 0),
        [pltpu.VMEM((6, rows, LANES), F32)],
    )(pos, conductivity, start, forcing, cond_field, materials)
    other = lax.ppermute(flip, "sx", flip_pairs)
    along = lax.ppermute(along, ("sx", "sy"), along_pairs)
    across = lax.ppermute(across, ("sx", "sy"), across_pairs)

    mine, send = call(window_kernel, [shape(2, WIDE, count, LANES)] * 2, (1, 0, 0, 0, 0))(pos, own, other, along, across)
    theirs = lax.ppermute(send, "sx", core_pairs)

    starts = jnp.stack([mine[:, :BLOCK], theirs[:, :BLOCK]])
    next_starts = lax.ppermute(starts, "slab", back)

    whole = shape(BLOCK, lines, LANES)
    flat = shape(lines, LANES)
    buffer = pltpu.VMEM((BLOCK, lines + 2 * BLOCK, LANES), F32)
    plain = pltpu.VMEM((BLOCK, lines, LANES), F32)
    ends = pltpu.VMEM((2, lines, LANES), F32)
    scaled = [plain] * 5 + [ends]
    states, south, north, east, west, base, sink = call(
        forward_kernel,
        [shape(STEPS * BLOCK, lines, LANES), whole, whole, whole, flat, whole, flat],
        (1, 1, 0, 0),
        [buffer, plain, buffer, plain, plain, buffer, buffer] + scaled,
        flops=20_000_000,
    )(pos, sink_rate, mine, theirs)

    pair = shape(2, BLOCK, count, LANES)
    weight, ends_here = call(defect_kernel, [whole, pair], (1, 0, 0, 0))(pos, states, next_starts[0], next_starts[1])
    defect = lax.ppermute(ends_here, "slab", forth)

    (adjoint,) = call(adjoint_kernel, [pair], (0,) * 8, [buffer, buffer, plain] + scaled, flops=10_000_000)(
        states, weight, south, north, east, west, base, sink
    )

    keep, send = call(swap_kernel, [pair] * 2, (1, 0, 0))(pos, adjoint, defect)
    got = lax.ppermute(send, "sx", core_pairs)
    keep, send = call(tile_kernel, [shape(2, rows, LANES)] * 2, (1, 0, 0))(pos, keep, got)
    got = lax.ppermute(send, "sx", flip_pairs)
    gradient, defect = call(join_kernel, [shape(rows, 2 * LANES)] * 2, (1, 0, 0))(pos, keep, got)
    return (defect[None], gradient[None])


def solution(mesh):
    placed = (P("slab", "sx", "sy"), P("slab", "sx", "sy"), P("sx", "sy"), P("sx", "sy"), P(), P())
    return jax.shard_map(
        functools.partial(per_device, mesh.shape["slab"], mesh.shape["sy"]),
        mesh=mesh,
        in_specs=placed,
        out_specs=(P("slab", "sx", "sy"), P("slab", "sx", "sy")),
        check_vma=False,
    )
```

```python
import functools

import jax
import jax.numpy as jnp
from jax import lax
from jax.experimental import pallas as pl
from jax.experimental.pallas import tpu as pltpu
from jax.sharding import PartitionSpec as P

BLOCK = 8
STEPS = 3
NEWTON = 2
JACOBI = 4
LANES = 128
HALO = 32
STRIP = LANES - 2 * HALO
CHUNK = 16

time_step = 2.0
half_step = 0.5 * time_step

VMEM = pl.BlockSpec(memory_space=pltpu.VMEM)
SMEM = pl.BlockSpec(memory_space=pltpu.SMEM)
HBM = pl.BlockSpec(memory_space=pltpu.HBM)
F32 = jnp.float32


def roll(x, shift):
    return pltpu.roll(x, shift % LANES, axis=x.ndim - 1)


def lanes_of(x):
    return lax.broadcasted_iota(jnp.int32, x.shape, x.ndim - 1)


def pick(test, a, b):
    return jnp.where(test, a, b)


TILE = 3 * BLOCK + 1
HALF = BLOCK + 1
WIDE = 4 * BLOCK + 1


def first_pack(s, f, k):
    at = lanes_of(s)
    far = jnp.where(at == 96, roll(s, 64), roll(k, 65))
    return jnp.where(at < 32, s, jnp.where(at < 64, roll(f, 32), jnp.where(at < 96, roll(k, 64), far)))


def last_pack(s, f, k):
    at = lanes_of(s)
    far = jnp.where(at == 96, roll(s, 1), roll(k, 2))
    return jnp.where(at < 32, roll(s, 32), jnp.where(at < 64, roll(f, 64), jnp.where(at < 96, roll(k, 96), far)))


def pack_kernel(pos, scales, start, source, cond, elements, own, flip, along, across, home, conductivity, materials, split, done):
    y = pos[0]
    copies = [pltpu.make_async_copy(scales, conductivity, done.at[7]), pltpu.make_async_copy(elements, materials, done.at[0])]
    for a, ref in enumerate((start, source, cond)):
        for half in range(2):
            part = ref.at[:, pl.ds(half * LANES, LANES)]
            copies.append(pltpu.make_async_copy(part, split.at[2 * a + half], done.at[1 + 2 * a + half]))
    for copy in copies:
        copy.start()
    count, cells = materials.shape
    width = start.shape[1]
    column = lax.broadcasted_iota(jnp.int32, (cells, width), 1)
    cell = lax.broadcasted_iota(jnp.int32, (cells, width), 0)
    spread = jnp.where(column // BLOCK == cell, 1.0, 0.0).astype(F32)
    copies[0].wait()
    copies[1].wait()
    material = jnp.dot(materials[...].astype(F32), spread, preferred_element_type=F32)
    is_gob = material > 0.5
    factor = jnp.where(is_gob, conductivity[1], conductivity[0])
    m0, m1 = material[:, :LANES], material[:, LANES:]
    lower = y == 0

    def place(p, tiles, packs):
        (first0, last0, first1, last1) = packs
        if tiles is not None:
            for a, (x0, x1) in enumerate(tiles):
                own[a * BLOCK + p] = pick(lower, x0, x1)
                flip[a * BLOCK + p] = pick(lower, x1, x0)
        own[TILE + p] = pick(lower, first1, last0)
        flip[TILE + p] = pick(lower, last0, first1)
        along[p] = pick(lower, last1, first0)
        across[p] = pick(lower, first0, last1)

    for copy in copies[2:]:
        copy.wait()
    home[0] = split[0]
    home[1] = split[1]
    for p in range(BLOCK):
        rows = pl.ds(p, count, stride=BLOCK)
        s0, s1, f0, f1, k0, k1 = (split[a, rows, :] for a in range(6))
        k0, k1 = k0 * factor[:, :LANES], k1 * factor[:, LANES:]
        packs = (first_pack(s0, f0, k0), last_pack(s0, f0, k0), first_pack(s1, f1, k1), last_pack(s1, f1, k1))
        place(p, ((s0, s1), (f0, f1), (k0, k1)), packs)
    own[3 * BLOCK] = pick(lower, m0, m1)
    flip[3 * BLOCK] = pick(lower, m1, m0)
    place(BLOCK, None, (m0, roll(m0, 32), m1, roll(m1, 32)))


def window_kernel(pos, own, other, along, across, mine, theirs):
    lower = pos[0] == 0
    even = pos[1] == 0
    at = lax.broadcasted_iota(jnp.int32, own.shape[1:], 1)

    def put(slot, index, left, right):
        mine[slot, index] = pick(even, left, right)
        theirs[slot, index] = pick(even, right, left)

    for slot, (tile, outer) in enumerate(((own, along), (other, across))):
        for p in range(BLOCK + 1):
            inner, far = tile[TILE + p], outer[p]
            west, east = pick(lower, far, inner), pick(lower, inner, far)
            if p == BLOCK:
                m = tile[3 * BLOCK]
                put(slot, 4 * BLOCK, jnp.where(at < 32, west, roll(m, 32)), jnp.where(at >= 96, roll(east, 96), roll(m, 96)))
                continue
            s, f, k = tile[p], tile[BLOCK + p], tile[2 * BLOCK + p]
            for a, x in enumerate((s, f, k)):
                left = jnp.where(at < 32, roll(west, -32 * a), roll(x, 32))
                right = jnp.where(at >= 96, roll(east, 96 - 32 * a), roll(x, 96))
                put(slot, a * BLOCK + p, left, right)
            left = jnp.where(at < 2, roll(west, 32), jnp.where(at == 127, roll(s, 31), roll(k, 30)))
            right = jnp.where(at == 0, roll(s, 97), jnp.where(at == 1, roll(k, 98), jnp.where(at == 127, roll(east, 31), roll(east, 29))))
            put(slot, 3 * BLOCK + p, left, right)


def chunks(lines):
    for first in range(0, lines, CHUNK):
        yield first


def shifted(ref, p, first, by):
    return ref[p, pl.ds(BLOCK + first + by, CHUNK), :]


def padded(ref, p, first):
    return ref[p, pl.ds(BLOCK + first, CHUNK), :]


def put_padded(ref, p, first, value):
    ref[p, pl.ds(BLOCK + first, CHUNK), :] = value


def clear_ends(ref, lines):
    zero = jnp.zeros((BLOCK, LANES), F32)
    for p in (0, BLOCK - 1):
        ref[p, 0:BLOCK, :] = zero
        ref[p, BLOCK + lines : 2 * BLOCK + lines, :] = zero


def factor_and_solve(first, diagonal, right, south, north, east, west, scaled, answer):
    at = pl.ds(first, CHUNK)
    keep_right, keep_south, keep_north, keep_lower, keep_upper, keep_ends = scaled
    values = []
    ratio = None
    value = None
    edge = None
    for p in range(BLOCK):
        pivot = diagonal(p)
        if p:
            pivot = pivot - edge * ratio
        inverse = 1.0 / pivot
        scaled_right = right(p) * inverse
        keep_right[p, at, :] = scaled_right
        keep_south[p, at, :] = south[p, at, :] * inverse
        keep_north[p, at, :] = north[p, at, :] * inverse
        if p == 0:
            keep_ends[0, at, :] = west[at, :] * inverse
            value = scaled_right
        else:
            lower = edge * inverse
            keep_lower[p, at, :] = lower
            value = scaled_right + lower * value
        edge = east[p, at, :]
        ratio = edge * inverse
        if p < BLOCK - 1:
            keep_upper[p, at, :] = ratio
        else:
            keep_ends[1, at, :] = ratio
        values.append(value)
    back_substitute(first, values, keep_upper, lambda p, z: put_padded(answer, p, first, z))


def back_substitute(first, values, upper, store):
    at = pl.ds(first, CHUNK)
    z = values[BLOCK - 1]
    store(BLOCK - 1, z)
    for p in range(BLOCK - 2, -1, -1):
        z = values[p] + upper[p, at, :] * z
        store(p, z)


def sweep(lines, scaled, old, store):
    keep_right, keep_south, keep_north, keep_lower, keep_upper, keep_ends = scaled
    for first in chunks(lines):
        at = pl.ds(first, CHUNK)
        values = []
        for p in range(BLOCK):
            z = padded(old, p, first)
            value = keep_right[p, at, :] + keep_south[p, at, :] * roll(z, 1) + keep_north[p, at, :] * roll(z, -1)
            if p == 0:
                value = value + keep_ends[0, at, :] * shifted(old, BLOCK - 1, first, -1)
            if p == BLOCK - 1:
                value = value + keep_ends[1, at, :] * shifted(old, 0, first, 1)
            if p:
                value = value + keep_lower[p, at, :] * values[-1]
            values.append(value)
        back_substitute(first, values, keep_upper, functools.partial(store, first))


def put_into(ref):
    return lambda first, p, z: put_padded(ref, p, first, z)


def forward_kernel(pos, sinks, mine, theirs, states, ends, south, north, east, west, base, sink, level, forcing, kappa, edge, previous, old, new, *scaled):
    y, c, strip, strips = pos[0], pos[1], pos[2], pos[3]
    lines = base.shape[1]
    count = mine.shape[2]
    for ref in (level, kappa, old, new):
        clear_ends(ref, lines)
    lane = lax.broadcasted_iota(jnp.int32, (count, LANES), 1)
    column = strip * STRIP - HALO + lane
    inside = (column >= 0) & (column < strips * STRIP)

    for ref, core in ((mine, c), (theirs, 1 - c)):
        for slot in range(2):
            chip = y if slot == 0 else 1 - y
            first = pl.multiple_of((2 * chip + core) * count, BLOCK)
            for p in range(BLOCK):
                level[p, pl.ds(BLOCK + first, count), :] = ref[slot, p]
                forcing[p, pl.ds(first, count), :] = time_step * ref[slot, BLOCK + p]
                kappa[p, pl.ds(BLOCK + first, count), :] = jnp.where(inside, ref[slot, 2 * BLOCK + p], 0.0)
                edge[p, pl.ds(first, count), :] = ref[slot, 3 * BLOCK + p]
            sink[pl.ds(first, count), :] = time_step * jnp.where(ref[slot, 4 * BLOCK] > 0.5, sinks[1], sinks[0])

    lane = lax.broadcasted_iota(jnp.int32, (CHUNK, LANES), 1)
    column = strip * STRIP - HALO + lane
    is_first = lane == 0
    is_last = lane == LANES - 1
    has_south = column != 0
    has_north = column != strips * STRIP - 1
    before = strip * STRIP - HALO > 0
    after = strip * STRIP - HALO + LANES < strips * STRIP

    for first in chunks(lines):
        at = pl.ds(first, CHUNK)
        k = [padded(kappa, p, first) for p in range(BLOCK)]
        wests = [half_step * (k[0] + shifted(kappa, BLOCK - 1, first, -1))]
        wests += [half_step * (k[p] + k[p - 1]) for p in range(1, BLOCK)]
        wests += [half_step * (k[BLOCK - 1] + shifted(kappa, 0, first, 1))]
        west[at, :] = wests[0]
        for p in range(BLOCK):
            side = edge[p, at, :]
            below = jnp.where(is_first, jnp.where(before, roll(side, -1), 0.0), roll(k[p], 1))
            above = jnp.where(is_last, jnp.where(after, roll(side, 1), 0.0), roll(k[p], -1))
            s = half_step * (k[p] + below)
            n = half_step * (k[p] + above)
            base[p, at, :] = 1.0 + (wests[p] + wests[p + 1] + s + n)
            south[p, at, :] = jnp.where(has_south, s, 0.0)
            north[p, at, :] = jnp.where(has_north, n, 0.0)
            east[p, at, :] = wests[p + 1]

    def newton(from_previous):
        for first in chunks(lines):
            at = pl.ds(first, CHUNK)
            sink_here = sink[at, :]
            tangents = {}
            currents = {}

            def state(p):
                if p not in currents:
                    currents[p] = padded(level, p, first)
                    tangents[p] = jnp.tanh(currents[p])
                return currents[p], tangents[p]

            def diagonal(p):
                _, tangent = state(p)
                return base[p, at, :] + sink_here * (1.0 - tangent * tangent)

            def right(p):
                current, tangent = state(p)
                side = edge[p, at, :]
                below = jnp.where(is_first, side, roll(current, 1))
                above = jnp.where(is_last, side, roll(current, -1))
                behind = padded(level, p - 1, first) if p else shifted(level, BLOCK - 1, first, -1)
                ahead = padded(level, p + 1, first) if p < BLOCK - 1 else shifted(level, 0, first, 1)
                behind_edge = east[p - 1, at, :] if p else west[at, :]
                pulled = (south[p, at, :] * below + north[p, at, :] * above + behind_edge * behind + east[p, at, :] * ahead)
                if from_previous:
                    held = (1.0 - base[p, at, :]) * current
                else:
                    held = previous[p, at, :] - base[p, at, :] * current
                return held + pulled - sink_here * tangent + forcing[p, at, :]

            factor_and_solve(first, diagonal, right, south, north, east, west, scaled, old)
        sweep(lines, scaled, old, put_into(new))
        sweep(lines, scaled, new, put_into(old))
        sweep(lines, scaled, old, lambda first, p, z: put_padded(level, p, first, padded(level, p, first) + z))

    def step(number, carry):
        for p in range(BLOCK):
            previous[p] = level[p, pl.ds(BLOCK, lines), :]
        newton(True)
        for _ in range(1, NEWTON):
            newton(False)
        for p in range(BLOCK):
            states[number * BLOCK + p] = level[p, pl.ds(BLOCK, lines), :]
        return carry

    lax.fori_loop(0, STEPS, step, 0)
    pack_strip(lambda p, first: level[p, pl.ds(BLOCK + first, count), :], ends)


def pack_strip(read, out):
    count = out.shape[2]
    at = lax.broadcasted_iota(jnp.int32, (count, LANES), 1)
    for core in range(2):
        for p in range(BLOCK):
            low, high = read(p, core * count), read(p, (2 + core) * count)
            out[core, p] = jnp.where(at < STRIP, roll(low, -HALO), roll(high, HALO))


def adjoint_kernel(pos, states, mine, theirs, south, north, east, west, base, sink, out, old, new, given, *scaled):
    y, c = pos[0], pos[1]
    lines = base.shape[1]
    count = mine.shape[2]
    for ref in (old, new):
        clear_ends(ref, lines)
    for ref, core in ((mine, c), (theirs, 1 - c)):
        for slot in range(2):
            chip = y if slot == 0 else 1 - y
            at = pl.ds(pl.multiple_of((2 * chip + core) * count, BLOCK), count)
            for p in range(BLOCK):
                given[p, at, :] = states[(STEPS - 1) * BLOCK + p, at, :] - ref[slot, p]

    def step(number, carry):
        level = STEPS - 1 - number
        for first in chunks(lines):
            at = pl.ds(first, CHUNK)
            sink_here = sink[at, :]

            def diagonal(p):
                tangent = jnp.tanh(states[level * BLOCK + p, at, :])
                return base[p, at, :] + sink_here * (1.0 - tangent * tangent)

            def right(p):
                return given[p, at, :]

            factor_and_solve(first, diagonal, right, south, north, east, west, scaled, old)
        sweep(lines, scaled, old, put_into(new))
        sweep(lines, scaled, new, put_into(old))

        def store(first, p, z):
            given[p, pl.ds(first, CHUNK), :] = z

        sweep(lines, scaled, old, store)
        return carry

    lax.fori_loop(0, STEPS, step, 0)
    pack_strip(lambda p, first: given[p, pl.ds(first, count), :], out)


def send_kernel(pos, adjoint, previous, keep, core, flip, both):
    y, c = pos[0], pos[1]
    count = adjoint.shape[2]
    at = lax.broadcasted_iota(jnp.int32, (count, LANES), 1)
    for p in range(BLOCK):
        rows = pl.ds(p, count, stride=BLOCK)
        for owner, (same, other) in ((c, (keep, flip)), (1 - c, (core, both))):
            a, e = adjoint[owner, p], previous[owner, p]
            chip0 = jnp.where(at < STRIP, a, roll(e, STRIP))
            chip1 = jnp.where(at < STRIP, roll(a, STRIP), e)
            same[rows, :] = pick(y == 0, chip0, chip1)
            other[rows, :] = pick(y == 0, chip1, chip0)


def join_kernel(pos, home, keep, core, flip, both, defect, gradient, built, done):
    y, c = pos[0], pos[1]
    at = lax.broadcasted_iota(jnp.int32, keep.shape, 1)
    copies = []
    for chip in range(2):
        here = y == chip
        one, two = pick(here, keep[...], flip[...]), pick(here, core[...], both[...])
        even, odd = pick(c == 0, one, two), pick(c == 0, two, one)
        missed = jnp.where(at < STRIP, roll(even, STRIP), odd) - home[chip]
        built[0, chip] = missed
        built[1, chip] = jnp.where(at < STRIP, even, roll(odd, STRIP)) - missed
        for a, out in enumerate((defect, gradient)):
            copies.append(pltpu.make_async_copy(built.at[a, chip], out.at[:, pl.ds(chip * LANES, LANES)], done.at[a, chip]))
            copies[-1].start()
    for copy in copies:
        copy.wait()


def per_device(slabs, strips_y, start_states, source, cond_field, materials, conductivity, sink_rate):
    sx = lax.axis_index("sx")
    z = lax.axis_index("sy")
    y, c = sx // 2, sx % 2
    pos = jnp.stack([y, c, 4 * z + sx, jnp.int32(4 * strips_y)]).astype(jnp.int32)
    start, forcing = start_states[0], source[0]
    rows = start.shape[0]
    count = rows // BLOCK
    lines = 4 * count
    shape = lambda *dims: jax.ShapeDtypeStruct(dims, F32)
    params = pltpu.CompilerParams(vmem_limit_bytes=48 * 1024 * 1024)

    def call(body, outs, ins, scratch=(), flops=0, out_specs=None):
        specs = [{"s": SMEM, "v": VMEM, "h": HBM}[kind] for kind in ins]
        cost = pl.CostEstimate(flops=flops, bytes_accessed=1 << 20, transcendentals=0)
        out_specs = out_specs or [VMEM] * len(outs)
        return pl.pallas_call(body, out_shape=outs, in_specs=specs, out_specs=out_specs, scratch_shapes=list(scratch), compiler_params=params, cost_estimate=cost)

    def joint(y_, c_, z_):
        return (2 * y_ + c_) * strips_y + z_

    everyone = [(a, b, d) for a in range(2) for b in range(2) for d in range(strips_y)]
    top = strips_y - 1

    def along_to(a, b, d):
        if a == 1:
            return (1, b, d - 1) if d > 0 else (0, b, d)
        return (0, b, d + 1) if d < top else (1, b, d)

    def across_to(a, b, d):
        if a == 1:
            return (0, b, d + 1) if d < top else (1, b, d)
        return (1, b, d - 1) if d > 0 else (0, b, d)

    along_pairs = [(joint(*v), joint(*along_to(*v))) for v in everyone]
    across_pairs = [(joint(*v), joint(*across_to(*v))) for v in everyone]
    flip_pairs = [(0, 2), (1, 3), (2, 0), (3, 1)]
    core_pairs = [(0, 1), (1, 0), (2, 3), (3, 2)]
    forth = [(i, (i + 1) % slabs) for i in range(slabs)]
    back = [(b, a) for a, b in forth]

    diagonal_pairs = [(0, 3), (1, 2), (2, 1), (3, 0)]

    own, flip, along, across, home = call(
        pack_kernel,
        [shape(TILE + HALF, count, LANES)] * 2 + [shape(HALF, count, LANES)] * 2 + [shape(2, rows, LANES)],
        "shhhhh",
        [pltpu.SMEM((2,), F32), pltpu.VMEM(materials.shape, jnp.int32), pltpu.VMEM((6, rows, LANES), F32), pltpu.SemaphoreType.DMA((8,))],
    )(pos, *(pltpu.with_memory_space_constraint(x, pltpu.HBM) for x in (conductivity, start, forcing, cond_field, materials)))
    other = lax.ppermute(flip, "sx", flip_pairs)
    along = lax.ppermute(along, ("sx", "sy"), along_pairs)
    across = lax.ppermute(across, ("sx", "sy"), across_pairs)

    mine, send = call(window_kernel, [shape(2, WIDE, count, LANES)] * 2, "svvvv")(pos, own, other, along, across)
    theirs = lax.ppermute(send, "sx", core_pairs)

    starts = jnp.stack([mine[:, :BLOCK], theirs[:, :BLOCK]])
    next_starts = lax.ppermute(starts, "slab", back)

    whole = shape(BLOCK, lines, LANES)
    flat = shape(lines, LANES)
    strip = shape(2, BLOCK, count, LANES)
    buffer = pltpu.VMEM((BLOCK, lines + 2 * BLOCK, LANES), F32)
    plain = pltpu.VMEM((BLOCK, lines, LANES), F32)
    scaled = [plain] * 5 + [pltpu.VMEM((2, lines, LANES), F32)]
    states, ends, south, north, east, west, base, sink = call(
        forward_kernel,
        [shape(STEPS * BLOCK, lines, LANES), strip, whole, whole, whole, flat, whole, flat],
        "ssvv",
        [buffer, plain, buffer, plain, plain, buffer, buffer] + scaled,
        flops=20_000_000,
    )(pos, sink_rate, mine, theirs)
    previous = lax.ppermute(ends, "slab", forth)

    (adjoint,) = call(adjoint_kernel, [strip], "s" + "v" * 9, [buffer, buffer, plain] + scaled, flops=10_000_000)(
        pos, states, next_starts[0], next_starts[1], south, north, east, west, base, sink
    )

    keep, core, flip, both = call(send_kernel, [shape(rows, LANES)] * 4, "svv")(pos, adjoint, previous)
    flip = lax.ppermute(flip, "sx", flip_pairs)
    both = lax.ppermute(both, "sx", diagonal_pairs)
    core = lax.ppermute(core, "sx", core_pairs)
    defect, gradient = call(
        join_kernel,
        [shape(rows, 2 * LANES)] * 2,
        "svvvvv",
        [pltpu.VMEM((2, 2, rows, LANES), F32), pltpu.SemaphoreType.DMA((2, 2))],
        out_specs=[HBM] * 2,
    )(pos, home, keep, core, flip, both)
    return (defect[None], gradient[None])


def solution(mesh):
    placed = (P("slab", "sx", "sy"), P("slab", "sx", "sy"), P("sx", "sy"), P("sx", "sy"), P(), P())
    return jax.shard_map(
        functools.partial(per_device, mesh.shape["slab"], mesh.shape["sy"]),
        mesh=mesh,
        in_specs=placed,
        out_specs=(P("slab", "sx", "sy"), P("slab", "sx", "sy")),
        check_vma=False,
    )
```

```python
import functools

import jax
import jax.numpy as jnp
from jax import lax
from jax.experimental import pallas as pl
from jax.experimental.pallas import tpu as pltpu
from jax.sharding import PartitionSpec as P

BLOCK = 8
STEPS = 3
NEWTON = 2
JACOBI = 4
LANES = 128
HALO = 32
STRIP = LANES - 2 * HALO
CHUNK = 16

time_step = 2.0
half_step = 0.5 * time_step

VMEM = pl.BlockSpec(memory_space=pltpu.VMEM)
SMEM = pl.BlockSpec(memory_space=pltpu.SMEM)
HBM = pl.BlockSpec(memory_space=pltpu.HBM)
F32 = jnp.float32


def roll(x, shift):
    return pltpu.roll(x, shift % LANES, axis=x.ndim - 1)


def lanes_of(x):
    return lax.broadcasted_iota(jnp.int32, x.shape, x.ndim - 1)


def position():
    sx = lax.axis_index("sx")
    return sx // 2, lax.rem(sx, 2), 4 * lax.axis_index("sy") + sx


def pick(test, a, b):
    return jnp.where(test, a, b)


TILE = 3 * BLOCK + 1
HALF = BLOCK + 1
WIDE = 4 * BLOCK + 1


def first_pack(s, f, k):
    at = lanes_of(s)
    far = jnp.where(at == 96, roll(s, 64), roll(k, 65))
    return jnp.where(at < 32, s, jnp.where(at < 64, roll(f, 32), jnp.where(at < 96, roll(k, 64), far)))


def last_pack(s, f, k):
    at = lanes_of(s)
    far = jnp.where(at == 96, roll(s, 1), roll(k, 2))
    return jnp.where(at < 32, roll(s, 32), jnp.where(at < 64, roll(f, 64), jnp.where(at < 96, roll(k, 96), far)))


def pack_kernel(scales, rates, start, source, cond, elements, own, flip, along, across, home, conductivity, sinks, materials, split, done):
    y, _, _ = position()
    copies = [pltpu.make_async_copy(scales, conductivity, done.at[7]), pltpu.make_async_copy(rates, sinks, done.at[8])]
    copies.append(pltpu.make_async_copy(elements, materials, done.at[0]))
    for a, ref in enumerate((start, source, cond)):
        for half in range(2):
            part = ref.at[:, pl.ds(half * LANES, LANES)]
            copies.append(pltpu.make_async_copy(part, split.at[2 * a + half], done.at[1 + 2 * a + half]))
    for copy in copies:
        copy.start()
    count, cells = materials.shape
    width = start.shape[1]
    column = lax.broadcasted_iota(jnp.int32, (cells, width), 1)
    cell = lax.broadcasted_iota(jnp.int32, (cells, width), 0)
    spread = jnp.where(column // BLOCK == cell, 1.0, 0.0).astype(F32)
    for copy in copies[:3]:
        copy.wait()
    material = jnp.dot(materials[...].astype(F32), spread, preferred_element_type=F32)
    is_gob = material > 0.5
    factor = jnp.where(is_gob, conductivity[1], conductivity[0])
    sink = time_step * jnp.where(is_gob, sinks[1], sinks[0])
    m0, m1 = sink[:, :LANES], sink[:, LANES:]
    lower = y == 0

    def place(p, tiles, packs):
        (first0, last0, first1, last1) = packs
        if tiles is not None:
            for a, (x0, x1) in enumerate(tiles):
                own[a * BLOCK + p] = pick(lower, x0, x1)
                flip[a * BLOCK + p] = pick(lower, x1, x0)
        own[TILE + p] = pick(lower, first1, last0)
        flip[TILE + p] = pick(lower, last0, first1)
        along[p] = pick(lower, last1, first0)
        across[p] = pick(lower, first0, last1)

    for copy in copies[3:]:
        copy.wait()
    home[0] = split[0]
    home[1] = split[1]
    for p in range(BLOCK):
        rows = pl.ds(p, count, stride=BLOCK)
        s0, s1, f0, f1, k0, k1 = (split[a, rows, :] for a in range(6))
        k0, k1 = k0 * factor[:, :LANES], k1 * factor[:, LANES:]
        packs = (first_pack(s0, f0, k0), last_pack(s0, f0, k0), first_pack(s1, f1, k1), last_pack(s1, f1, k1))
        place(p, ((s0, s1), (f0, f1), (k0, k1)), packs)
    own[3 * BLOCK] = pick(lower, m0, m1)
    flip[3 * BLOCK] = pick(lower, m1, m0)
    place(BLOCK, None, (m0, roll(m0, 32), m1, roll(m1, 32)))


def window_kernel(own, other, along, across, mine, theirs, rest, beside, done):
    y, c, _ = position()
    lower, even = y == 0, c == 0
    at = lax.broadcasted_iota(jnp.int32, own.shape[1:], 1)

    def put(slot, index, left, right):
        mine[slot, index] = pick(even, left, right)
        theirs[slot, index] = pick(even, right, left)

    for p in range(BLOCK):
        west0, east0 = pick(lower, along[p], own[TILE + p]), pick(lower, own[TILE + p], along[p])
        west1, east1 = pick(lower, across[p], other[TILE + p]), pick(lower, other[TILE + p], across[p])
        high = jnp.where(at < 96, roll(west1, 64), roll(east1, 96))
        beside[p] = jnp.where(at < 32, west0, jnp.where(at < 64, roll(east0, 32), high))
    parts = ((other.at[pl.ds(0, BLOCK)], 0), (beside, 1))
    copies = [pltpu.make_async_copy(part, rest.at[pl.ds(i * BLOCK, BLOCK)], done.at[i]) for part, i in parts]
    for copy in copies:
        copy.start()
    for slot, (tile, outer) in enumerate(((own, along), (other, across))):
        for p in range(BLOCK + 1):
            inner, far = tile[TILE + p], outer[p]
            west, east = pick(lower, far, inner), pick(lower, inner, far)
            if p == BLOCK:
                m = tile[3 * BLOCK]
                put(slot, 4 * BLOCK, jnp.where(at < 32, west, roll(m, 32)), jnp.where(at >= 96, roll(east, 96), roll(m, 96)))
                continue
            s, f, k = tile[p], tile[BLOCK + p], tile[2 * BLOCK + p]
            for a, x in enumerate((s, f, k)):
                left = jnp.where(at < 32, roll(west, -32 * a), roll(x, 32))
                right = jnp.where(at >= 96, roll(east, 96 - 32 * a), roll(x, 96))
                put(slot, a * BLOCK + p, left, right)
            left = jnp.where(at < 2, roll(west, 32), jnp.where(at == 127, roll(s, 31), roll(k, 30)))
            right = jnp.where(at == 0, roll(s, 97), jnp.where(at == 1, roll(k, 98), jnp.where(at == 127, roll(east, 31), roll(east, 29))))
            put(slot, 3 * BLOCK + p, left, right)
    for copy in copies:
        copy.wait()


def chunks(lines):
    for first in range(0, lines, CHUNK):
        yield first


def shifted(ref, p, first, by):
    return ref[p, pl.ds(BLOCK + first + by, CHUNK), :]


def padded(ref, p, first):
    return ref[p, pl.ds(BLOCK + first, CHUNK), :]


def put_padded(ref, p, first, value):
    ref[p, pl.ds(BLOCK + first, CHUNK), :] = value


def clear_ends(ref, lines):
    zero = jnp.zeros((BLOCK, LANES), F32)
    for p in (0, BLOCK - 1):
        ref[p, 0:BLOCK, :] = zero
        ref[p, BLOCK + lines : 2 * BLOCK + lines, :] = zero


def factor_and_solve(first, diagonal, right, south, north, east, west, scaled, answer):
    at = pl.ds(first, CHUNK)
    keep_right, keep_south, keep_north, keep_lower, keep_upper, keep_ends = scaled
    values = []
    ratio = None
    value = None
    edge = None
    for p in range(BLOCK):
        pivot = diagonal(p)
        if p:
            pivot = pivot - edge * ratio
        inverse = 1.0 / pivot
        scaled_right = right(p) * inverse
        keep_right[p, at, :] = scaled_right
        keep_south[p, at, :] = south[p, at, :] * inverse
        keep_north[p, at, :] = north[p, at, :] * inverse
        if p == 0:
            keep_ends[0, at, :] = west[at, :] * inverse
            value = scaled_right
        else:
            lower = edge * inverse
            keep_lower[p, at, :] = lower
            value = scaled_right + lower * value
        edge = east[p, at, :]
        ratio = edge * inverse
        if p < BLOCK - 1:
            keep_upper[p, at, :] = ratio
        else:
            keep_ends[1, at, :] = ratio
        values.append(value)
    back_substitute(first, values, keep_upper, lambda p, z: put_padded(answer, p, first, z))


def back_substitute(first, values, upper, store):
    at = pl.ds(first, CHUNK)
    z = values[BLOCK - 1]
    store(BLOCK - 1, z)
    for p in range(BLOCK - 2, -1, -1):
        z = values[p] + upper[p, at, :] * z
        store(p, z)


def sweep(lines, scaled, old, store):
    keep_right, keep_south, keep_north, keep_lower, keep_upper, keep_ends = scaled
    for first in chunks(lines):
        at = pl.ds(first, CHUNK)
        values = []
        for p in range(BLOCK):
            z = padded(old, p, first)
            value = keep_right[p, at, :] + keep_south[p, at, :] * roll(z, 1) + keep_north[p, at, :] * roll(z, -1)
            if p == 0:
                value = value + keep_ends[0, at, :] * shifted(old, BLOCK - 1, first, -1)
            if p == BLOCK - 1:
                value = value + keep_ends[1, at, :] * shifted(old, 0, first, 1)
            if p:
                value = value + keep_lower[p, at, :] * values[-1]
            values.append(value)
        back_substitute(first, values, keep_upper, functools.partial(store, first))


def put_into(ref):
    return lambda first, p, z: put_padded(ref, p, first, z)


def forward_kernel(strips, mine, theirs, states, ends, south, north, east, west, base, sink, level, forcing, kappa, edge, previous, old, new, *scaled):
    y, c, strip = position()
    lines = base.shape[1]
    count = mine.shape[2]
    for ref in (level, kappa, old, new):
        clear_ends(ref, lines)
    lane = lax.broadcasted_iota(jnp.int32, (count, LANES), 1)
    column = strip * STRIP - HALO + lane
    inside = (column >= 0) & (column < strips * STRIP)

    for ref, core in ((mine, c), (theirs, 1 - c)):
        for slot in range(2):
            chip = y if slot == 0 else 1 - y
            first = pl.multiple_of((2 * chip + core) * count, BLOCK)
            for p in range(BLOCK):
                level[p, pl.ds(BLOCK + first, count), :] = ref[slot, p]
                forcing[p, pl.ds(first, count), :] = time_step * ref[slot, BLOCK + p]
                kappa[p, pl.ds(BLOCK + first, count), :] = jnp.where(inside, ref[slot, 2 * BLOCK + p], 0.0)
                edge[p, pl.ds(first, count), :] = ref[slot, 3 * BLOCK + p]
            sink[pl.ds(first, count), :] = ref[slot, 4 * BLOCK]

    lane = lax.broadcasted_iota(jnp.int32, (CHUNK, LANES), 1)
    column = strip * STRIP - HALO + lane
    is_first = lane == 0
    is_last = lane == LANES - 1
    has_south = column != 0
    has_north = column != strips * STRIP - 1
    before = strip * STRIP - HALO > 0
    after = strip * STRIP - HALO + LANES < strips * STRIP

    for first in chunks(lines):
        at = pl.ds(first, CHUNK)
        k = [padded(kappa, p, first) for p in range(BLOCK)]
        wests = [half_step * (k[0] + shifted(kappa, BLOCK - 1, first, -1))]
        wests += [half_step * (k[p] + k[p - 1]) for p in range(1, BLOCK)]
        wests += [half_step * (k[BLOCK - 1] + shifted(kappa, 0, first, 1))]
        west[at, :] = wests[0]
        for p in range(BLOCK):
            side = edge[p, at, :]
            below = jnp.where(is_first, jnp.where(before, roll(side, -1), 0.0), roll(k[p], 1))
            above = jnp.where(is_last, jnp.where(after, roll(side, 1), 0.0), roll(k[p], -1))
            s = half_step * (k[p] + below)
            n = half_step * (k[p] + above)
            base[p, at, :] = 1.0 + (wests[p] + wests[p + 1] + s + n)
            south[p, at, :] = jnp.where(has_south, s, 0.0)
            north[p, at, :] = jnp.where(has_north, n, 0.0)
            east[p, at, :] = wests[p + 1]

    def newton(from_previous):
        for first in chunks(lines):
            at = pl.ds(first, CHUNK)
            sink_here = sink[at, :]
            tangents = {}
            currents = {}

            def state(p):
                if p not in currents:
                    currents[p] = padded(level, p, first)
                    tangents[p] = jnp.tanh(currents[p])
                return currents[p], tangents[p]

            def diagonal(p):
                _, tangent = state(p)
                return base[p, at, :] + sink_here * (1.0 - tangent * tangent)

            def right(p):
                current, tangent = state(p)
                side = edge[p, at, :]
                below = jnp.where(is_first, side, roll(current, 1))
                above = jnp.where(is_last, side, roll(current, -1))
                behind = padded(level, p - 1, first) if p else shifted(level, BLOCK - 1, first, -1)
                ahead = padded(level, p + 1, first) if p < BLOCK - 1 else shifted(level, 0, first, 1)
                behind_edge = east[p - 1, at, :] if p else west[at, :]
                pulled = (south[p, at, :] * below + north[p, at, :] * above + behind_edge * behind + east[p, at, :] * ahead)
                if from_previous:
                    held = (1.0 - base[p, at, :]) * current
                else:
                    held = previous[p, at, :] - base[p, at, :] * current
                return held + pulled - sink_here * tangent + forcing[p, at, :]

            factor_and_solve(first, diagonal, right, south, north, east, west, scaled, old)
        sweep(lines, scaled, old, put_into(new))
        sweep(lines, scaled, new, put_into(old))
        sweep(lines, scaled, old, lambda first, p, z: put_padded(level, p, first, padded(level, p, first) + z))

    def step(number, carry):
        for p in range(BLOCK):
            previous[p] = level[p, pl.ds(BLOCK, lines), :]
        newton(True)
        for _ in range(1, NEWTON):
            newton(False)
        for p in range(BLOCK):
            states[number * BLOCK + p] = level[p, pl.ds(BLOCK, lines), :]
        return carry

    lax.fori_loop(0, STEPS, step, 0)
    pack_strip(lambda p, first: level[p, pl.ds(BLOCK + first, count), :], ends, True)


def pack_strip(read, out, swapped=False):
    count = out.shape[2]
    at = lax.broadcasted_iota(jnp.int32, (count, LANES), 1)
    for core in range(2):
        for p in range(BLOCK):
            low, high = read(p, core * count), read(p, (2 + core) * count)
            if swapped:
                low, high = high, low
            out[core, p] = jnp.where(at < STRIP, roll(low, -HALO), roll(high, HALO))


def adjoint_kernel(states, own, rest, their_own, their_rest, south, north, east, west, base, sink, out, old, new, given, *scaled):
    y, c, _ = position()
    lines = base.shape[1]
    count = own.shape[1]
    for ref in (old, new):
        clear_ends(ref, lines)
    lane = lax.broadcasted_iota(jnp.int32, (count, LANES), 1)
    even = c == 0
    turn = jnp.where(even, HALO, LANES - HALO)
    edge = jnp.where(even, lane, lane - (LANES - HALO))
    from_side = (edge >= 0) & (edge < HALO)
    for first_tile, others, core in ((own, rest, c), (their_own, their_rest, 1 - c)):
        for slot in range(2):
            chip = y if slot == 0 else 1 - y
            at = pl.ds(pl.multiple_of((2 * chip + core) * count, BLOCK), count)
            side_turn = jnp.where(even, (LANES - 2 * HALO * slot) % LANES, (2 * LANES - 2 * HALO - 2 * HALO * slot) % LANES)
            for p in range(BLOCK):
                tile = pltpu.roll((others if slot else first_tile)[p], turn, axis=1)
                side = pltpu.roll(others[BLOCK + p], side_turn, axis=1)
                start = jnp.where(from_side, side, tile)
                given[p, at, :] = states[(STEPS - 1) * BLOCK + p, at, :] - start

    def step(number, carry):
        level = STEPS - 1 - number
        for first in chunks(lines):
            at = pl.ds(first, CHUNK)
            sink_here = sink[at, :]

            def diagonal(p):
                tangent = jnp.tanh(states[level * BLOCK + p, at, :])
                return base[p, at, :] + sink_here * (1.0 - tangent * tangent)

            def right(p):
                return given[p, at, :]

            factor_and_solve(first, diagonal, right, south, north, east, west, scaled, old)
        sweep(lines, scaled, old, put_into(new))
        sweep(lines, scaled, new, put_into(old))

        def store(first, p, z):
            given[p, pl.ds(first, CHUNK), :] = z

        sweep(lines, scaled, old, store)
        return carry

    lax.fori_loop(0, STEPS, step, 0)
    pack_strip(lambda p, first: given[p, pl.ds(first, count), :], out)


def join_kernel(home, keep, core, flip, both, defect, gradient, built, done):
    y, c, _ = position()
    count = keep.shape[1]
    at = lax.broadcasted_iota(jnp.int32, (count, LANES), 1)
    copies = []
    for chip in range(2):
        here = y == chip
        for p in range(BLOCK):
            one, two = pick(here, keep[p], flip[p]), pick(here, core[p], both[p])
            even, odd = pick(c == 0, one, two), pick(c == 0, two, one)
            low, high = jnp.where(at < STRIP, even, roll(odd, STRIP)), jnp.where(at < STRIP, roll(even, STRIP), odd)
            rows = pl.ds(p, count, stride=BLOCK)
            missed = pick(y == 0, high, low) - home[chip, rows, :]
            built[0, chip, rows, :] = missed
            built[1, chip, rows, :] = pick(y == 0, low, high) - missed
        for a, out in enumerate((defect, gradient)):
            copies.append(pltpu.make_async_copy(built.at[a, chip], out.at[:, pl.ds(chip * LANES, LANES)], done.at[a, chip]))
            copies[-1].start()
    for copy in copies:
        copy.wait()


def per_device(slabs, strips_y, start_states, source, cond_field, materials, conductivity, sink_rate):
    sx = lax.axis_index("sx")
    y, c = sx // 2, sx % 2
    start, forcing = start_states[0], source[0]
    rows = start.shape[0]
    count = rows // BLOCK
    lines = 4 * count
    shape = lambda *dims: jax.ShapeDtypeStruct(dims, F32)
    params = pltpu.CompilerParams(vmem_limit_bytes=16 * 1024 * 1024)

    def call(body, outs, ins, scratch=(), flops=0, out_specs=None):
        specs = [{"s": SMEM, "v": VMEM, "h": HBM}[kind] for kind in ins]
        cost = pl.CostEstimate(flops=flops, bytes_accessed=1 << 20, transcendentals=0)
        out_specs = out_specs or [VMEM] * len(outs)
        return pl.pallas_call(body, out_shape=outs, in_specs=specs, out_specs=out_specs, scratch_shapes=list(scratch), compiler_params=params, cost_estimate=cost)

    def joint(y_, c_, z_):
        return (2 * y_ + c_) * strips_y + z_

    everyone = [(a, b, d) for a in range(2) for b in range(2) for d in range(strips_y)]
    top = strips_y - 1

    def along_to(a, b, d):
        if a == 1:
            return (1, b, d - 1) if d > 0 else (0, b, d)
        return (0, b, d + 1) if d < top else (1, b, d)

    def across_to(a, b, d):
        if a == 1:
            return (0, b, d + 1) if d < top else (0, b, 0)
        return (1, b, d - 1) if d > 0 else (1, b, top)

    along_pairs = [(joint(*v), joint(*along_to(*v))) for v in everyone]
    across_pairs = [(joint(*v), joint(*across_to(*v))) for v in everyone]
    flip_pairs = [(0, 2), (1, 3), (2, 0), (3, 1)]
    core_pairs = [(0, 1), (1, 0), (2, 3), (3, 2)]
    forth = [(i, (i + 1) % slabs) for i in range(slabs)]
    back = [(b, a) for a, b in forth]

    both_pairs = [(s * 4 + a, (s - 1) % slabs * 4 + b) for s in range(slabs) for a, b in core_pairs]
    diagonal_pairs = [(0, 3), (1, 2), (2, 1), (3, 0)]

    own, flip, along, across, home = call(
        pack_kernel,
        [shape(TILE + HALF, count, LANES)] * 2 + [shape(HALF, count, LANES)] * 2 + [shape(2, rows, LANES)],
        "hhhhhh",
        [pltpu.SMEM((2,), F32), pltpu.SMEM((2,), F32), pltpu.VMEM(materials.shape, jnp.int32), pltpu.VMEM((6, rows, LANES), F32), pltpu.SemaphoreType.DMA((9,))],
    )(*(pltpu.with_memory_space_constraint(x, pltpu.HBM) for x in (conductivity, sink_rate, start, forcing, cond_field, materials)))
    other = lax.ppermute(flip, "sx", flip_pairs)
    along = lax.ppermute(along, ("sx", "sy"), along_pairs)
    across = lax.ppermute(across, ("sx", "sy"), across_pairs)

    next_own = lax.ppermute(own[:BLOCK], "slab", back)
    other, along, across, next_own = lax.optimization_barrier((other, along, across, next_own))
    mine, send, rest = call(
        window_kernel,
        [shape(2, WIDE, count, LANES)] * 2 + [shape(2 * BLOCK, count, LANES)],
        "vvvv",
        [pltpu.VMEM((BLOCK, count, LANES), F32), pltpu.SemaphoreType.DMA((2,))],
        out_specs=[VMEM, VMEM, HBM],
    )(own, other, along, across)
    theirs = lax.ppermute(send, "sx", core_pairs)

    their_own = lax.ppermute(next_own, "sx", core_pairs)
    next_rest = lax.ppermute(rest, "slab", back)
    their_rest = lax.ppermute(rest, ("slab", "sx"), both_pairs)

    theirs, their_own = lax.optimization_barrier((theirs, their_own))

    whole = shape(BLOCK, lines, LANES)
    flat = shape(lines, LANES)
    strip = shape(2, BLOCK, count, LANES)
    buffer = pltpu.VMEM((BLOCK, lines + 2 * BLOCK, LANES), F32)
    plain = pltpu.VMEM((BLOCK, lines, LANES), F32)
    scaled = [plain] * 5 + [pltpu.VMEM((2, lines, LANES), F32)]
    states, ends, south, north, east, west, base, sink = call(
        functools.partial(forward_kernel, 4 * strips_y),
        [shape(STEPS * BLOCK, lines, LANES), strip, whole, whole, whole, flat, whole, flat],
        "vv",
        [buffer, plain, buffer, plain, plain, buffer, buffer] + scaled,
        flops=20_000_000,
    )(mine, theirs)
    previous = lax.ppermute(ends, "slab", forth)
    (adjoint,) = call(adjoint_kernel, [strip], "v" * 11, [buffer, buffer, plain] + scaled, flops=10_000_000)(
        states, next_own, next_rest, their_own, their_rest, south, north, east, west, base, sink
    )

    low_lanes = lax.broadcasted_iota(jnp.int32, (BLOCK, count, LANES), 2) < STRIP

    def strip_for(chip, owner):
        a = lax.dynamic_index_in_dim(adjoint, owner, 0, keepdims=False)
        e = lax.dynamic_index_in_dim(previous, owner, 0, keepdims=False)
        return jnp.where(low_lanes == (chip == 0), a, e)

    keep, core, flip, both = (strip_for(*to) for to in ((y, c), (y, 1 - c), (1 - y, c), (1 - y, 1 - c)))
    flip = lax.ppermute(flip, "sx", flip_pairs)
    both = lax.ppermute(both, "sx", diagonal_pairs)
    core = lax.ppermute(core, "sx", core_pairs)
    defect, gradient = call(
        join_kernel,
        [shape(rows, 2 * LANES)] * 2,
        "vvvvv",
        [pltpu.VMEM((2, 2, rows, LANES), F32), pltpu.SemaphoreType.DMA((2, 2))],
        out_specs=[HBM] * 2,
    )(home, keep, core, flip, both)
    return (defect[None], gradient[None])


def solution(mesh):
    placed = (P("slab", "sx", "sy"), P("slab", "sx", "sy"), P("sx", "sy"), P("sx", "sy"), P(), P())
    return jax.shard_map(
        functools.partial(per_device, mesh.shape["slab"], mesh.shape["sy"]),
        mesh=mesh,
        in_specs=placed,
        out_specs=(P("slab", "sx", "sy"), P("slab", "sx", "sy")),
        check_vma=False,
    )
```

```python
import functools

import jax
import jax.numpy as jnp
from jax import lax
from jax.experimental import pallas as pl
from jax.experimental.pallas import tpu as pltpu
from jax.sharding import PartitionSpec as P

BLOCK = 8
STEPS = 3
NEWTON = 2
JACOBI = 4
LANES = 128
HALO = 32
STRIP = LANES - 2 * HALO
CHUNK = 16

time_step = 2.0
half_step = 0.5 * time_step

VMEM = pl.BlockSpec(memory_space=pltpu.VMEM)
SMEM = pl.BlockSpec(memory_space=pltpu.SMEM)
HBM = pl.BlockSpec(memory_space=pltpu.HBM)
F32 = jnp.float32


def roll(x, shift):
    return pltpu.roll(x, shift % LANES, axis=x.ndim - 1)


def lanes_of(x):
    return lax.broadcasted_iota(jnp.int32, x.shape, x.ndim - 1)


def position():
    sx = lax.axis_index("sx")
    return sx // 2, lax.rem(sx, 2), 4 * lax.axis_index("sy") + sx


def pick(test, a, b):
    return jnp.where(test, a, b)


TILE = 3 * BLOCK + 1
HALF = BLOCK + 1
WIDE = 4 * BLOCK + 1


def first_pack(s, f, k):
    at = lanes_of(s)
    far = jnp.where(at == 96, roll(s, 64), roll(k, 65))
    return jnp.where(at < 32, s, jnp.where(at < 64, roll(f, 32), jnp.where(at < 96, roll(k, 64), far)))


def last_pack(s, f, k):
    at = lanes_of(s)
    far = jnp.where(at == 96, roll(s, 1), roll(k, 2))
    return jnp.where(at < 32, roll(s, 32), jnp.where(at < 64, roll(f, 64), jnp.where(at < 96, roll(k, 96), far)))


def pack_kernel(scales, rates, start, source, cond, elements, own, flip, along, across, home, conductivity, sinks, materials, split, done):
    y, _, _ = position()
    copies = [pltpu.make_async_copy(scales, conductivity, done.at[7]), pltpu.make_async_copy(rates, sinks, done.at[8])]
    copies.append(pltpu.make_async_copy(elements, materials, done.at[0]))
    for a, ref in enumerate((start, source, cond)):
        for half in range(2):
            part = ref.at[:, pl.ds(half * LANES, LANES)]
            copies.append(pltpu.make_async_copy(part, split.at[2 * a + half], done.at[1 + 2 * a + half]))
    for copy in copies:
        copy.start()
    count, cells = materials.shape
    width = start.shape[1]
    column = lax.broadcasted_iota(jnp.int32, (cells, width), 1)
    cell = lax.broadcasted_iota(jnp.int32, (cells, width), 0)
    spread = jnp.where(column // BLOCK == cell, 1.0, 0.0).astype(F32)
    for copy in copies[:3]:
        copy.wait()
    material = jnp.dot(materials[...].astype(F32), spread, preferred_element_type=F32)
    is_gob = material > 0.5
    factor = jnp.where(is_gob, conductivity[1], conductivity[0])
    sink = time_step * jnp.where(is_gob, sinks[1], sinks[0])
    m0, m1 = sink[:, :LANES], sink[:, LANES:]
    lower = y == 0

    def place(p, tiles, packs):
        (first0, last0, first1, last1) = packs
        if tiles is not None:
            for a, (x0, x1) in enumerate(tiles):
                own[a * BLOCK + p] = pick(lower, x0, x1)
                flip[a * BLOCK + p] = pick(lower, x1, x0)
        own[TILE + p] = pick(lower, first1, last0)
        flip[TILE + p] = pick(lower, last0, first1)
        along[p] = pick(lower, last1, first0)
        across[p] = pick(lower, first0, last1)

    for copy in copies[3:]:
        copy.wait()
    home[0] = split[0]
    home[1] = split[1]
    for p in range(BLOCK):
        rows = pl.ds(p, count, stride=BLOCK)
        s0, s1, f0, f1, k0, k1 = (split[a, rows, :] for a in range(6))
        k0, k1 = k0 * factor[:, :LANES], k1 * factor[:, LANES:]
        packs = (first_pack(s0, f0, k0), last_pack(s0, f0, k0), first_pack(s1, f1, k1), last_pack(s1, f1, k1))
        place(p, ((s0, s1), (f0, f1), (k0, k1)), packs)
    own[3 * BLOCK] = pick(lower, m0, m1)
    flip[3 * BLOCK] = pick(lower, m1, m0)
    place(BLOCK, None, (m0, roll(m0, 32), m1, roll(m1, 32)))


def window_kernel(own, other, along, across, mine, theirs, rest, beside, done):
    y, c, _ = position()
    lower, even = y == 0, c == 0
    at = lax.broadcasted_iota(jnp.int32, own.shape[1:], 1)

    def put(slot, index, left, right):
        mine[slot, index] = pick(even, left, right)
        theirs[slot, index] = pick(even, right, left)

    for p in range(BLOCK):
        west0, east0 = pick(lower, along[p], own[TILE + p]), pick(lower, own[TILE + p], along[p])
        west1, east1 = pick(lower, across[p], other[TILE + p]), pick(lower, other[TILE + p], across[p])
        high = jnp.where(at < 96, roll(west1, 64), roll(east1, 96))
        beside[p] = jnp.where(at < 32, west0, jnp.where(at < 64, roll(east0, 32), high))
    parts = ((other.at[pl.ds(0, BLOCK)], 0), (beside, 1))
    copies = [pltpu.make_async_copy(part, rest.at[pl.ds(i * BLOCK, BLOCK)], done.at[i]) for part, i in parts]
    for copy in copies:
        copy.start()
    for slot, (tile, outer) in enumerate(((own, along), (other, across))):
        for p in range(BLOCK + 1):
            inner, far = tile[TILE + p], outer[p]
            west, east = pick(lower, far, inner), pick(lower, inner, far)
            if p == BLOCK:
                m = tile[3 * BLOCK]
                put(slot, 4 * BLOCK, jnp.where(at < 32, west, roll(m, 32)), jnp.where(at >= 96, roll(east, 96), roll(m, 96)))
                continue
            s, f, k = tile[p], tile[BLOCK + p], tile[2 * BLOCK + p]
            for a, x in enumerate((s, f, k)):
                left = jnp.where(at < 32, roll(west, -32 * a), roll(x, 32))
                right = jnp.where(at >= 96, roll(east, 96 - 32 * a), roll(x, 96))
                put(slot, a * BLOCK + p, left, right)
            left = jnp.where(at < 2, roll(west, 32), jnp.where(at == 127, roll(s, 31), roll(k, 30)))
            right = jnp.where(at == 0, roll(s, 97), jnp.where(at == 1, roll(k, 98), jnp.where(at == 127, roll(east, 31), roll(east, 29))))
            put(slot, 3 * BLOCK + p, left, right)
    for copy in copies:
        copy.wait()


def chunks(lines):
    for first in range(0, lines, CHUNK):
        yield first


def shifted(ref, p, first, by):
    return ref[p, pl.ds(BLOCK + first + by, CHUNK), :]


def padded(ref, p, first):
    return ref[p, pl.ds(BLOCK + first, CHUNK), :]


def put_padded(ref, p, first, value):
    ref[p, pl.ds(BLOCK + first, CHUNK), :] = value


def clear_ends(ref, lines):
    zero = jnp.zeros((BLOCK, LANES), F32)
    for p in (0, BLOCK - 1):
        ref[p, 0:BLOCK, :] = zero
        ref[p, BLOCK + lines : 2 * BLOCK + lines, :] = zero


def factor_and_solve(first, diagonal, right, south, north, east, west, scaled, answer):
    at = pl.ds(first, CHUNK)
    keep_right, keep_south, keep_north, keep_lower, keep_upper, keep_ends = scaled
    values = []
    ratio = None
    value = None
    edge = None
    for p in range(BLOCK):
        pivot = diagonal(p)
        if p:
            pivot = pivot - edge * ratio
        inverse = 1.0 / pivot
        scaled_right = right(p) * inverse
        keep_right[p, at, :] = scaled_right
        keep_south[p, at, :] = south[p, at, :] * inverse
        keep_north[p, at, :] = north[p, at, :] * inverse
        if p == 0:
            keep_ends[0, at, :] = west[at, :] * inverse
            value = scaled_right
        else:
            lower = edge * inverse
            keep_lower[p, at, :] = lower
            value = scaled_right + lower * value
        edge = east[p, at, :]
        ratio = edge * inverse
        if p < BLOCK - 1:
            keep_upper[p, at, :] = ratio
        else:
            keep_ends[1, at, :] = ratio
        values.append(value)
    back_substitute(first, values, keep_upper, lambda p, z: put_padded(answer, p, first, z))


def back_substitute(first, values, upper, store):
    at = pl.ds(first, CHUNK)
    z = values[BLOCK - 1]
    store(BLOCK - 1, z)
    for p in range(BLOCK - 2, -1, -1):
        z = values[p] + upper[p, at, :] * z
        store(p, z)


def sweep(lines, scaled, old, store):
    keep_right, keep_south, keep_north, keep_lower, keep_upper, keep_ends = scaled
    for first in chunks(lines):
        at = pl.ds(first, CHUNK)
        values = []
        for p in range(BLOCK):
            z = padded(old, p, first)
            value = keep_right[p, at, :] + keep_south[p, at, :] * roll(z, 1) + keep_north[p, at, :] * roll(z, -1)
            if p == 0:
                value = value + keep_ends[0, at, :] * shifted(old, BLOCK - 1, first, -1)
            if p == BLOCK - 1:
                value = value + keep_ends[1, at, :] * shifted(old, 0, first, 1)
            if p:
                value = value + keep_lower[p, at, :] * values[-1]
            values.append(value)
        back_substitute(first, values, keep_upper, functools.partial(store, first))


def put_into(ref):
    return lambda first, p, z: put_padded(ref, p, first, z)


def forward_kernel(strips, mine, theirs, states, ends, south, north, east, west, base, sink, level, forcing, kappa, edge, previous, old, new, *scaled):
    y, c, strip = position()
    lines = base.shape[1]
    count = mine.shape[2]
    for ref in (level, kappa, old, new):
        clear_ends(ref, lines)
    lane = lax.broadcasted_iota(jnp.int32, (count, LANES), 1)
    column = strip * STRIP - HALO + lane
    inside = (column >= 0) & (column < strips * STRIP)

    for ref, core in ((mine, c), (theirs, 1 - c)):
        for slot in range(2):
            chip = y if slot == 0 else 1 - y
            first = pl.multiple_of((2 * chip + core) * count, BLOCK)
            for p in range(BLOCK):
                level[p, pl.ds(BLOCK + first, count), :] = ref[slot, p]
                forcing[p, pl.ds(first, count), :] = time_step * ref[slot, BLOCK + p]
                kappa[p, pl.ds(BLOCK + first, count), :] = jnp.where(inside, ref[slot, 2 * BLOCK + p], 0.0)
                edge[p, pl.ds(first, count), :] = ref[slot, 3 * BLOCK + p]
            sink[pl.ds(first, count), :] = ref[slot, 4 * BLOCK]

    lane = lax.broadcasted_iota(jnp.int32, (CHUNK, LANES), 1)
    column = strip * STRIP - HALO + lane
    is_first = lane == 0
    is_last = lane == LANES - 1
    has_south = column != 0
    has_north = column != strips * STRIP - 1
    before = strip * STRIP - HALO > 0
    after = strip * STRIP - HALO + LANES < strips * STRIP

    for first in chunks(lines):
        at = pl.ds(first, CHUNK)
        k = [padded(kappa, p, first) for p in range(BLOCK)]
        wests = [half_step * (k[0] + shifted(kappa, BLOCK - 1, first, -1))]
        wests += [half_step * (k[p] + k[p - 1]) for p in range(1, BLOCK)]
        wests += [half_step * (k[BLOCK - 1] + shifted(kappa, 0, first, 1))]
        west[at, :] = wests[0]
        for p in range(BLOCK):
            side = edge[p, at, :]
            below = jnp.where(is_first, jnp.where(before, roll(side, -1), 0.0), roll(k[p], 1))
            above = jnp.where(is_last, jnp.where(after, roll(side, 1), 0.0), roll(k[p], -1))
            s = half_step * (k[p] + below)
            n = half_step * (k[p] + above)
            base[p, at, :] = 1.0 + (wests[p] + wests[p + 1] + s + n)
            south[p, at, :] = jnp.where(has_south, s, 0.0)
            north[p, at, :] = jnp.where(has_north, n, 0.0)
            east[p, at, :] = wests[p + 1]

    def newton(from_previous):
        for first in chunks(lines):
            at = pl.ds(first, CHUNK)
            sink_here = sink[at, :]
            tangents = {}
            currents = {}

            def state(p):
                if p not in currents:
                    currents[p] = padded(level, p, first)
                    tangents[p] = jnp.tanh(currents[p])
                return currents[p], tangents[p]

            def diagonal(p):
                _, tangent = state(p)
                return base[p, at, :] + sink_here * (1.0 - tangent * tangent)

            def right(p):
                current, tangent = state(p)
                side = edge[p, at, :]
                below = jnp.where(is_first, side, roll(current, 1))
                above = jnp.where(is_last, side, roll(current, -1))
                behind = padded(level, p - 1, first) if p else shifted(level, BLOCK - 1, first, -1)
                ahead = padded(level, p + 1, first) if p < BLOCK - 1 else shifted(level, 0, first, 1)
                behind_edge = east[p - 1, at, :] if p else west[at, :]
                pulled = (south[p, at, :] * below + north[p, at, :] * above + behind_edge * behind + east[p, at, :] * ahead)
                if from_previous:
                    held = (1.0 - base[p, at, :]) * current
                else:
                    held = previous[p, at, :] - base[p, at, :] * current
                return held + pulled - sink_here * tangent + forcing[p, at, :]

            factor_and_solve(first, diagonal, right, south, north, east, west, scaled, old)
        sweep(lines, scaled, old, put_into(new))
        sweep(lines, scaled, new, put_into(old))
        sweep(lines, scaled, old, lambda first, p, z: put_padded(level, p, first, padded(level, p, first) + z))

    def step(number, carry):
        for p in range(BLOCK):
            previous[p] = level[p, pl.ds(BLOCK, lines), :]
        newton(True)
        for _ in range(1, NEWTON):
            newton(False)
        for p in range(BLOCK):
            states[number * BLOCK + p] = level[p, pl.ds(BLOCK, lines), :]
        return carry

    lax.fori_loop(0, STEPS, step, 0)
    pack_strip(lambda p, first: level[p, pl.ds(BLOCK + first, count), :], ends, True)


def pack_strip(read, out, swapped=False):
    count = out.shape[2]
    at = lax.broadcasted_iota(jnp.int32, (count, LANES), 1)
    for core in range(2):
        for p in range(BLOCK):
            low, high = read(p, core * count), read(p, (2 + core) * count)
            if swapped:
                low, high = high, low
            out[core, p] = jnp.where(at < STRIP, roll(low, -HALO), roll(high, HALO))


def adjoint_kernel(states, own, rest, their_own, their_rest, south, north, east, west, base, sink, out, old, new, given, *scaled):
    y, c, _ = position()
    lines = base.shape[1]
    count = own.shape[1]
    for ref in (old, new):
        clear_ends(ref, lines)
    lane = lax.broadcasted_iota(jnp.int32, (count, LANES), 1)
    even = c == 0
    turn = jnp.where(even, HALO, LANES - HALO)
    edge = jnp.where(even, lane, lane - (LANES - HALO))
    from_side = (edge >= 0) & (edge < HALO)
    for first_tile, others, core in ((own, rest, c), (their_own, their_rest, 1 - c)):
        for slot in range(2):
            chip = y if slot == 0 else 1 - y
            at = pl.ds(pl.multiple_of((2 * chip + core) * count, BLOCK), count)
            side_turn = jnp.where(even, (LANES - 2 * HALO * slot) % LANES, (2 * LANES - 2 * HALO - 2 * HALO * slot) % LANES)
            for p in range(BLOCK):
                tile = pltpu.roll((others if slot else first_tile)[p], turn, axis=1)
                side = pltpu.roll(others[BLOCK + p], side_turn, axis=1)
                start = jnp.where(from_side, side, tile)
                given[p, at, :] = states[(STEPS - 1) * BLOCK + p, at, :] - start

    def step(number, carry):
        level = STEPS - 1 - number
        for first in chunks(lines):
            at = pl.ds(first, CHUNK)
            sink_here = sink[at, :]

            def diagonal(p):
                tangent = jnp.tanh(states[level * BLOCK + p, at, :])
                return base[p, at, :] + sink_here * (1.0 - tangent * tangent)

            def right(p):
                return given[p, at, :]

            factor_and_solve(first, diagonal, right, south, north, east, west, scaled, old)
        sweep(lines, scaled, old, put_into(new))
        sweep(lines, scaled, new, put_into(old))

        def store(first, p, z):
            given[p, pl.ds(first, CHUNK), :] = z

        sweep(lines, scaled, old, store)
        return carry

    lax.fori_loop(0, STEPS, step, 0)
    pack_strip(lambda p, first: given[p, pl.ds(first, count), :], out)


def join_kernel(home, keep, core, flip, both, defect, gradient, built, done):
    y, c, _ = position()
    count = keep.shape[1]
    at = lax.broadcasted_iota(jnp.int32, (count, LANES), 1)
    copies = []
    for chip in range(2):
        here = y == chip
        for p in range(BLOCK):
            one, two = pick(here, keep[p], flip[p]), pick(here, core[p], both[p])
            even, odd = pick(c == 0, one, two), pick(c == 0, two, one)
            low, high = jnp.where(at < STRIP, even, roll(odd, STRIP)), jnp.where(at < STRIP, roll(even, STRIP), odd)
            rows = pl.ds(p, count, stride=BLOCK)
            missed = pick(y == 0, high, low) - home[chip, rows, :]
            built[0, chip, rows, :] = missed
            built[1, chip, rows, :] = pick(y == 0, low, high) - missed
        for a, out in enumerate((defect, gradient)):
            copies.append(pltpu.make_async_copy(built.at[a, chip], out.at[:, pl.ds(chip * LANES, LANES)], done.at[a, chip]))
            copies[-1].start()
    for copy in copies:
        copy.wait()


def per_device(slabs, strips_y, start_states, source, cond_field, materials, conductivity, sink_rate):
    sx = lax.axis_index("sx")
    y, c = sx // 2, sx % 2
    start, forcing = start_states[0], source[0]
    rows = start.shape[0]
    count = rows // BLOCK
    lines = 4 * count
    shape = lambda *dims: jax.ShapeDtypeStruct(dims, F32)
    params = pltpu.CompilerParams(vmem_limit_bytes=16 * 1024 * 1024)

    def call(body, outs, ins, scratch=(), flops=0, out_specs=None):
        specs = [{"s": SMEM, "v": VMEM, "h": HBM}[kind] for kind in ins]
        cost = pl.CostEstimate(flops=flops, bytes_accessed=1 << 20, transcendentals=0)
        out_specs = out_specs or [VMEM] * len(outs)
        return pl.pallas_call(body, out_shape=outs, in_specs=specs, out_specs=out_specs, scratch_shapes=list(scratch), compiler_params=params, cost_estimate=cost)

    def joint(y_, c_, z_):
        return (2 * y_ + c_) * strips_y + z_

    everyone = [(a, b, d) for a in range(2) for b in range(2) for d in range(strips_y)]
    top = strips_y - 1

    def along_to(a, b, d):
        if a == 1:
            return (1, b, d - 1) if d > 0 else (0, b, d)
        return (0, b, d + 1) if d < top else (1, b, d)

    def across_to(a, b, d):
        if a == 1:
            return (0, b, d + 1) if d < top else (1, 1 - b, d)
        return (1, b, d - 1) if d > 0 else (0, 1 - b, d)

    along_pairs = [(joint(*v), joint(*along_to(*v))) for v in everyone]
    across_pairs = [(joint(*v), joint(*across_to(*v))) for v in everyone]
    flip_pairs = [(0, 2), (1, 3), (2, 0), (3, 1)]
    core_pairs = [(0, 1), (1, 0), (2, 3), (3, 2)]
    forth = [(i, (i + 1) % slabs) for i in range(slabs)]
    back = [(b, a) for a, b in forth]

    both_pairs = [(s * 4 + a, (s - 1) % slabs * 4 + b) for s in range(slabs) for a, b in core_pairs]
    diagonal_pairs = [(0, 3), (1, 2), (2, 1), (3, 0)]

    own, flip, along, across, home = call(
        pack_kernel,
        [shape(TILE + HALF, count, LANES)] * 2 + [shape(HALF, count, LANES)] * 2 + [shape(2, rows, LANES)],
        "hhhhhh",
        [pltpu.SMEM((2,), F32), pltpu.SMEM((2,), F32), pltpu.VMEM(materials.shape, jnp.int32), pltpu.VMEM((6, rows, LANES), F32), pltpu.SemaphoreType.DMA((9,))],
    )(*(pltpu.with_memory_space_constraint(x, pltpu.HBM) for x in (conductivity, sink_rate, start, forcing, cond_field, materials)))
    other = lax.ppermute(flip, "sx", flip_pairs)
    along = lax.ppermute(along, ("sx", "sy"), along_pairs)
    across = lax.ppermute(across, ("sx", "sy"), across_pairs)

    next_own = lax.ppermute(own[:BLOCK], "slab", back)
    other, along, across, next_own = lax.optimization_barrier((other, along, across, next_own))
    mine, send, rest = call(
        window_kernel,
        [shape(2, WIDE, count, LANES)] * 2 + [shape(2 * BLOCK, count, LANES)],
        "vvvv",
        [pltpu.VMEM((BLOCK, count, LANES), F32), pltpu.SemaphoreType.DMA((2,))],
        out_specs=[VMEM, VMEM, HBM],
    )(own, other, along, across)
    theirs = lax.ppermute(send, "sx", core_pairs)

    their_own = lax.ppermute(next_own, "sx", core_pairs)
    next_rest = lax.ppermute(rest, "slab", back)
    their_rest = lax.ppermute(rest, ("slab", "sx"), both_pairs)

    theirs, their_own = lax.optimization_barrier((theirs, their_own))

    whole = shape(BLOCK, lines, LANES)
    flat = shape(lines, LANES)
    strip = shape(2, BLOCK, count, LANES)
    buffer = pltpu.VMEM((BLOCK, lines + 2 * BLOCK, LANES), F32)
    plain = pltpu.VMEM((BLOCK, lines, LANES), F32)
    scaled = [plain] * 5 + [pltpu.VMEM((2, lines, LANES), F32)]
    states, ends, south, north, east, west, base, sink = call(
        functools.partial(forward_kernel, 4 * strips_y),
        [shape(STEPS * BLOCK, lines, LANES), strip, whole, whole, whole, flat, whole, flat],
        "vv",
        [buffer, plain, buffer, plain, plain, buffer, buffer] + scaled,
        flops=20_000_000,
    )(mine, theirs)
    previous = lax.ppermute(ends, "slab", forth)
    (adjoint,) = call(adjoint_kernel, [strip], "v" * 11, [buffer, buffer, plain] + scaled, flops=10_000_000)(
        states, next_own, next_rest, their_own, their_rest, south, north, east, west, base, sink
    )

    low_lanes = lax.broadcasted_iota(jnp.int32, (BLOCK, count, LANES), 2) < STRIP

    def strip_for(chip, owner):
        a = lax.dynamic_index_in_dim(adjoint, owner, 0, keepdims=False)
        e = lax.dynamic_index_in_dim(previous, owner, 0, keepdims=False)
        return jnp.where(low_lanes == (chip == 0), a, e)

    keep, core, flip, both = (strip_for(*to) for to in ((y, c), (y, 1 - c), (1 - y, c), (1 - y, 1 - c)))
    flip = lax.ppermute(flip, "sx", flip_pairs)
    both = lax.ppermute(both, "sx", diagonal_pairs)
    core = lax.ppermute(core, "sx", core_pairs)
    defect, gradient = call(
        join_kernel,
        [shape(rows, 2 * LANES)] * 2,
        "vvvvv",
        [pltpu.VMEM((2, 2, rows, LANES), F32), pltpu.SemaphoreType.DMA((2, 2))],
        out_specs=[HBM] * 2,
    )(home, keep, core, flip, both)
    return (defect[None], gradient[None])


def solution(mesh):
    placed = (P("slab", "sx", "sy"), P("slab", "sx", "sy"), P("sx", "sy"), P("sx", "sy"), P(), P())
    return jax.shard_map(
        functools.partial(per_device, mesh.shape["slab"], mesh.shape["sy"]),
        mesh=mesh,
        in_specs=placed,
        out_specs=(P("slab", "sx", "sy"), P("slab", "sx", "sy")),
        check_vma=False,
    )
```

```python
import functools

import jax
import jax.numpy as jnp
from jax import lax
from jax.experimental import pallas as pl
from jax.experimental.pallas import tpu as pltpu
from jax.sharding import PartitionSpec as P

BLOCK = 8
STEPS = 3
NEWTON = 2
JACOBI = 4
LANES = 128
HALO = 32
STRIP = LANES - 2 * HALO
CHUNK = 16

time_step = 2.0
half_step = 0.5 * time_step

VMEM = pl.BlockSpec(memory_space=pltpu.VMEM)
SMEM = pl.BlockSpec(memory_space=pltpu.SMEM)
HBM = pl.BlockSpec(memory_space=pltpu.HBM)
F32 = jnp.float32


def roll(x, shift):
    return pltpu.roll(x, shift % LANES, axis=x.ndim - 1)


def lanes_of(x):
    return lax.broadcasted_iota(jnp.int32, x.shape, x.ndim - 1)


def position():
    sx = lax.axis_index("sx")
    return sx // 2, lax.rem(sx, 2), 4 * lax.axis_index("sy") + sx


def pick(test, a, b):
    return jnp.where(test, a, b)


TILE = 3 * BLOCK + 1
HALF = BLOCK + 1
WIDE = 4 * BLOCK + 1


def first_pack(s, f, k):
    at = lanes_of(s)
    far = jnp.where(at == 96, roll(s, 64), roll(k, 65))
    return jnp.where(at < 32, s, jnp.where(at < 64, roll(f, 32), jnp.where(at < 96, roll(k, 64), far)))


def last_pack(s, f, k):
    at = lanes_of(s)
    far = jnp.where(at == 96, roll(s, 1), roll(k, 2))
    return jnp.where(at < 32, roll(s, 32), jnp.where(at < 64, roll(f, 64), jnp.where(at < 96, roll(k, 96), far)))


def pack_kernel(scales, rates, start, source, cond, elements, own, flip, along, across, home, conductivity, sinks, materials, split, done):
    y, _, _ = position()
    copies = [pltpu.make_async_copy(scales, conductivity, done.at[7]), pltpu.make_async_copy(rates, sinks, done.at[8])]
    copies.append(pltpu.make_async_copy(elements, materials, done.at[0]))
    for a, ref in enumerate((start, source, cond)):
        for half in range(2):
            part = ref.at[:, pl.ds(half * LANES, LANES)]
            copies.append(pltpu.make_async_copy(part, split.at[2 * a + half], done.at[1 + 2 * a + half]))
    for copy in copies:
        copy.start()
    count, cells = materials.shape
    width = start.shape[1]
    column = lax.broadcasted_iota(jnp.int32, (cells, width), 1)
    cell = lax.broadcasted_iota(jnp.int32, (cells, width), 0)
    spread = jnp.where(column // BLOCK == cell, 1.0, 0.0).astype(F32)
    for copy in copies[:3]:
        copy.wait()
    material = jnp.dot(materials[...].astype(F32), spread, preferred_element_type=F32)
    is_gob = material > 0.5
    factor = jnp.where(is_gob, conductivity[1], conductivity[0])
    sink = time_step * jnp.where(is_gob, sinks[1], sinks[0])
    m0, m1 = sink[:, :LANES], sink[:, LANES:]
    lower = y == 0

    def place(p, tiles, packs):
        (first0, last0, first1, last1) = packs
        if tiles is not None:
            for a, (x0, x1) in enumerate(tiles):
                own[a * BLOCK + p] = pick(lower, x0, x1)
                flip[a * BLOCK + p] = pick(lower, x1, x0)
        own[TILE + p] = pick(lower, first1, last0)
        flip[TILE + p] = pick(lower, last0, first1)
        along[p] = pick(lower, last1, first0)
        across[p] = pick(lower, first0, last1)

    for copy in copies[3:]:
        copy.wait()
    home[0] = split[0]
    home[1] = split[1]
    for p in range(BLOCK):
        rows = pl.ds(p, count, stride=BLOCK)
        s0, s1, f0, f1, k0, k1 = (split[a, rows, :] for a in range(6))
        k0, k1 = k0 * factor[:, :LANES], k1 * factor[:, LANES:]
        packs = (first_pack(s0, f0, k0), last_pack(s0, f0, k0), first_pack(s1, f1, k1), last_pack(s1, f1, k1))
        place(p, ((s0, s1), (f0, f1), (k0, k1)), packs)
    own[3 * BLOCK] = pick(lower, m0, m1)
    flip[3 * BLOCK] = pick(lower, m1, m0)
    place(BLOCK, None, (m0, roll(m0, 32), m1, roll(m1, 32)))


def window_kernel(own, other, along, across, mine, theirs, rest, beside, done):
    y, c, _ = position()
    lower, even = y == 0, c == 0
    at = lax.broadcasted_iota(jnp.int32, own.shape[1:], 1)

    def put(slot, index, left, right):
        mine[slot, index] = pick(even, left, right)
        theirs[slot, index] = pick(even, right, left)

    for p in range(BLOCK):
        west0, east0 = pick(lower, along[p], own[TILE + p]), pick(lower, own[TILE + p], along[p])
        west1, east1 = pick(lower, across[p], other[TILE + p]), pick(lower, other[TILE + p], across[p])
        high = jnp.where(at < 96, roll(west1, 64), roll(east1, 96))
        beside[p] = jnp.where(at < 32, west0, jnp.where(at < 64, roll(east0, 32), high))
    parts = ((other.at[pl.ds(0, BLOCK)], 0), (beside, 1))
    copies = [pltpu.make_async_copy(part, rest.at[pl.ds(i * BLOCK, BLOCK)], done.at[i]) for part, i in parts]
    for copy in copies:
        copy.start()
    for slot, (tile, outer) in enumerate(((own, along), (other, across))):
        for p in range(BLOCK + 1):
            inner, far = tile[TILE + p], outer[p]
            west, east = pick(lower, far, inner), pick(lower, inner, far)
            if p == BLOCK:
                m = tile[3 * BLOCK]
                put(slot, 4 * BLOCK, jnp.where(at < 32, west, roll(m, 32)), jnp.where(at >= 96, roll(east, 96), roll(m, 96)))
                continue
            s, f, k = tile[p], tile[BLOCK + p], tile[2 * BLOCK + p]
            for a, x in enumerate((s, f, k)):
                left = jnp.where(at < 32, roll(west, -32 * a), roll(x, 32))
                right = jnp.where(at >= 96, roll(east, 96 - 32 * a), roll(x, 96))
                put(slot, a * BLOCK + p, left, right)
            left = jnp.where(at < 2, roll(west, 32), jnp.where(at == 127, roll(s, 31), roll(k, 30)))
            right = jnp.where(at == 0, roll(s, 97), jnp.where(at == 1, roll(k, 98), jnp.where(at == 127, roll(east, 31), roll(east, 29))))
            put(slot, 3 * BLOCK + p, left, right)
    for copy in copies:
        copy.wait()


def chunks(lines):
    for first in range(0, lines, CHUNK):
        yield first


def shifted(ref, p, first, by):
    return ref[p, pl.ds(BLOCK + first + by, CHUNK), :]


def padded(ref, p, first):
    return ref[p, pl.ds(BLOCK + first, CHUNK), :]


def put_padded(ref, p, first, value):
    ref[p, pl.ds(BLOCK + first, CHUNK), :] = value


def clear_ends(ref, lines):
    zero = jnp.zeros((BLOCK, LANES), F32)
    for p in (0, BLOCK - 1):
        ref[p, 0:BLOCK, :] = zero
        ref[p, BLOCK + lines : 2 * BLOCK + lines, :] = zero


def factor_and_solve(first, diagonal, right, south, north, east, west, scaled, answer):
    at = pl.ds(first, CHUNK)
    keep_right, keep_south, keep_north, keep_lower, keep_upper, keep_ends = scaled
    values = []
    ratio = None
    value = None
    edge = None
    for p in range(BLOCK):
        pivot = diagonal(p)
        if p:
            pivot = pivot - edge * ratio
        inverse = 1.0 / pivot
        scaled_right = right(p) * inverse
        keep_right[p, at, :] = scaled_right
        keep_south[p, at, :] = south[p, at, :] * inverse
        keep_north[p, at, :] = north[p, at, :] * inverse
        if p == 0:
            keep_ends[0, at, :] = west[at, :] * inverse
            value = scaled_right
        else:
            lower = edge * inverse
            keep_lower[p, at, :] = lower
            value = scaled_right + lower * value
        edge = east[p, at, :]
        ratio = edge * inverse
        if p < BLOCK - 1:
            keep_upper[p, at, :] = ratio
        else:
            keep_ends[1, at, :] = ratio
        values.append(value)
    back_substitute(first, values, keep_upper, lambda p, z: put_padded(answer, p, first, z))


def back_substitute(first, values, upper, store):
    at = pl.ds(first, CHUNK)
    z = values[BLOCK - 1]
    store(BLOCK - 1, z)
    for p in range(BLOCK - 2, -1, -1):
        z = values[p] + upper[p, at, :] * z
        store(p, z)


def sweep(lines, scaled, old, store):
    keep_right, keep_south, keep_north, keep_lower, keep_upper, keep_ends = scaled
    for first in chunks(lines):
        at = pl.ds(first, CHUNK)
        values = []
        for p in range(BLOCK):
            z = padded(old, p, first)
            value = keep_right[p, at, :] + keep_south[p, at, :] * roll(z, 1) + keep_north[p, at, :] * roll(z, -1)
            if p == 0:
                value = value + keep_ends[0, at, :] * shifted(old, BLOCK - 1, first, -1)
            if p == BLOCK - 1:
                value = value + keep_ends[1, at, :] * shifted(old, 0, first, 1)
            if p:
                value = value + keep_lower[p, at, :] * values[-1]
            values.append(value)
        back_substitute(first, values, keep_upper, functools.partial(store, first))


def put_into(ref):
    return lambda first, p, z: put_padded(ref, p, first, z)


def forward_kernel(strips, mine, theirs, states, ends, south, north, east, west, base, sink, level, forcing, kappa, edge, previous, old, new, *scaled):
    y, c, strip = position()
    lines = base.shape[1]
    count = mine.shape[2]
    for ref in (level, kappa, old, new):
        clear_ends(ref, lines)
    lane = lax.broadcasted_iota(jnp.int32, (count, LANES), 1)
    column = strip * STRIP - HALO + lane
    inside = (column >= 0) & (column < strips * STRIP)

    for ref, core in ((mine, c), (theirs, 1 - c)):
        for slot in range(2):
            chip = y if slot == 0 else 1 - y
            first = pl.multiple_of((2 * chip + core) * count, BLOCK)
            for p in range(BLOCK):
                level[p, pl.ds(BLOCK + first, count), :] = ref[slot, p]
                forcing[p, pl.ds(first, count), :] = time_step * ref[slot, BLOCK + p]
                kappa[p, pl.ds(BLOCK + first, count), :] = jnp.where(inside, ref[slot, 2 * BLOCK + p], 0.0)
                edge[p, pl.ds(first, count), :] = ref[slot, 3 * BLOCK + p]
            sink[pl.ds(first, count), :] = ref[slot, 4 * BLOCK]

    lane = lax.broadcasted_iota(jnp.int32, (CHUNK, LANES), 1)
    column = strip * STRIP - HALO + lane
    is_first = lane == 0
    is_last = lane == LANES - 1
    has_south = column != 0
    has_north = column != strips * STRIP - 1
    before = strip * STRIP - HALO > 0
    after = strip * STRIP - HALO + LANES < strips * STRIP

    for first in chunks(lines):
        at = pl.ds(first, CHUNK)
        k = [padded(kappa, p, first) for p in range(BLOCK)]
        wests = [half_step * (k[0] + shifted(kappa, BLOCK - 1, first, -1))]
        wests += [half_step * (k[p] + k[p - 1]) for p in range(1, BLOCK)]
        wests += [half_step * (k[BLOCK - 1] + shifted(kappa, 0, first, 1))]
        west[at, :] = wests[0]
        for p in range(BLOCK):
            side = edge[p, at, :]
            below = jnp.where(is_first, jnp.where(before, roll(side, -1), 0.0), roll(k[p], 1))
            above = jnp.where(is_last, jnp.where(after, roll(side, 1), 0.0), roll(k[p], -1))
            s = half_step * (k[p] + below)
            n = half_step * (k[p] + above)
            base[p, at, :] = 1.0 + (wests[p] + wests[p + 1] + s + n)
            south[p, at, :] = jnp.where(has_south, s, 0.0)
            north[p, at, :] = jnp.where(has_north, n, 0.0)
            east[p, at, :] = wests[p + 1]

    def newton(from_previous, store):
        for first in chunks(lines):
            at = pl.ds(first, CHUNK)
            sink_here = sink[at, :]
            tangents = {}
            currents = {}

            def state(p):
                if p not in currents:
                    currents[p] = padded(level, p, first)
                    tangents[p] = jnp.tanh(currents[p])
                return currents[p], tangents[p]

            def diagonal(p):
                _, tangent = state(p)
                return base[p, at, :] + sink_here * (1.0 - tangent * tangent)

            def right(p):
                current, tangent = state(p)
                below, above = roll(current, 1), roll(current, -1)
                if from_previous:
                    side = edge[p, at, :]
                    below, above = jnp.where(is_first, side, below), jnp.where(is_last, side, above)
                behind = padded(level, p - 1, first) if p else shifted(level, BLOCK - 1, first, -1)
                ahead = padded(level, p + 1, first) if p < BLOCK - 1 else shifted(level, 0, first, 1)
                behind_edge = east[p - 1, at, :] if p else west[at, :]
                pulled = (south[p, at, :] * below + north[p, at, :] * above + behind_edge * behind + east[p, at, :] * ahead)
                if from_previous:
                    held = current + forcing[p, at, :]
                    previous[p, at, :] = held
                else:
                    held = previous[p, at, :]
                return held - base[p, at, :] * current + pulled - sink_here * tangent

            factor_and_solve(first, diagonal, right, south, north, east, west, scaled, old)
        sweep(lines, scaled, old, put_into(new))
        sweep(lines, scaled, new, put_into(old))
        sweep(lines, scaled, old, store)

    def step(number, carry):
        def store(keep, first, p, z):
            value = padded(level, p, first) + z
            put_padded(level, p, first, value)
            if keep:
                states[number * BLOCK + p, pl.ds(first, CHUNK), :] = value

        for turn in range(NEWTON):
            newton(turn == 0, functools.partial(store, turn == NEWTON - 1))
        return carry

    lax.fori_loop(0, STEPS, step, 0)
    pack_strip(lambda p, first: level[p, pl.ds(BLOCK + first, count), :], ends, True)


def pack_strip(read, out, swapped=False):
    count = out.shape[2]
    at = lax.broadcasted_iota(jnp.int32, (count, LANES), 1)
    for core in range(2):
        for p in range(BLOCK):
            low, high = read(p, core * count), read(p, (2 + core) * count)
            if swapped:
                low, high = high, low
            out[core, p] = jnp.where(at < STRIP, roll(low, -HALO), roll(high, HALO))


def adjoint_kernel(states, own, rest, their_own, their_rest, south, north, east, west, base, sink, out, old, new, given, *scaled):
    y, c, _ = position()
    lines = base.shape[1]
    count = own.shape[1]
    for ref in (old, new):
        clear_ends(ref, lines)
    lane = lax.broadcasted_iota(jnp.int32, (count, LANES), 1)
    even = c == 0
    turn = jnp.where(even, HALO, LANES - HALO)
    edge = jnp.where(even, lane, lane - (LANES - HALO))
    from_side = (edge >= 0) & (edge < HALO)
    for first_tile, others, core in ((own, rest, c), (their_own, their_rest, 1 - c)):
        for slot in range(2):
            chip = y if slot == 0 else 1 - y
            at = pl.ds(pl.multiple_of((2 * chip + core) * count, BLOCK), count)
            side_turn = jnp.where(even, (LANES - 2 * HALO * slot) % LANES, (2 * LANES - 2 * HALO - 2 * HALO * slot) % LANES)
            for p in range(BLOCK):
                tile = pltpu.roll((others if slot else first_tile)[p], turn, axis=1)
                side = pltpu.roll(others[BLOCK + p], side_turn, axis=1)
                start = jnp.where(from_side, side, tile)
                given[p, at, :] = states[(STEPS - 1) * BLOCK + p, at, :] - start

    def step(number, carry):
        level = STEPS - 1 - number
        for first in chunks(lines):
            at = pl.ds(first, CHUNK)
            sink_here = sink[at, :]

            def diagonal(p):
                tangent = jnp.tanh(states[level * BLOCK + p, at, :])
                return base[p, at, :] + sink_here * (1.0 - tangent * tangent)

            def right(p):
                return given[p, at, :]

            factor_and_solve(first, diagonal, right, south, north, east, west, scaled, old)
        sweep(lines, scaled, old, put_into(new))
        sweep(lines, scaled, new, put_into(old))

        def store(first, p, z):
            given[p, pl.ds(first, CHUNK), :] = z

        sweep(lines, scaled, old, store)
        return carry

    lax.fori_loop(0, STEPS, step, 0)
    pack_strip(lambda p, first: given[p, pl.ds(first, count), :], out)


def join_kernel(home, keep, core, flip, both, defect, gradient, built, done):
    y, c, _ = position()
    count = keep.shape[1]
    at = lax.broadcasted_iota(jnp.int32, (count, LANES), 1)
    copies = []
    for chip in range(2):
        here = y == chip
        for p in range(BLOCK):
            one, two = pick(here, keep[p], flip[p]), pick(here, core[p], both[p])
            even, odd = pick(c == 0, one, two), pick(c == 0, two, one)
            low, high = jnp.where(at < STRIP, even, roll(odd, STRIP)), jnp.where(at < STRIP, roll(even, STRIP), odd)
            rows = pl.ds(p, count, stride=BLOCK)
            missed = pick(y == 0, high, low) - home[chip, rows, :]
            built[0, chip, rows, :] = missed
            built[1, chip, rows, :] = pick(y == 0, low, high) - missed
        for a, out in enumerate((defect, gradient)):
            copies.append(pltpu.make_async_copy(built.at[a, chip], out.at[:, pl.ds(chip * LANES, LANES)], done.at[a, chip]))
            copies[-1].start()
    for copy in copies:
        copy.wait()


def per_device(slabs, strips_y, start_states, source, cond_field, materials, conductivity, sink_rate):
    sx = lax.axis_index("sx")
    y, c = sx // 2, sx % 2
    start, forcing = start_states[0], source[0]
    rows = start.shape[0]
    count = rows // BLOCK
    lines = 4 * count
    shape = lambda *dims: jax.ShapeDtypeStruct(dims, F32)
    params = pltpu.CompilerParams(vmem_limit_bytes=16 * 1024 * 1024)

    def call(body, outs, ins, scratch=(), flops=0, out_specs=None):
        specs = [{"s": SMEM, "v": VMEM, "h": HBM}[kind] for kind in ins]
        cost = pl.CostEstimate(flops=flops, bytes_accessed=1 << 20, transcendentals=0)
        out_specs = out_specs or [VMEM] * len(outs)
        return pl.pallas_call(body, out_shape=outs, in_specs=specs, out_specs=out_specs, scratch_shapes=list(scratch), compiler_params=params, cost_estimate=cost)

    def joint(y_, c_, z_):
        return (2 * y_ + c_) * strips_y + z_

    everyone = [(a, b, d) for a in range(2) for b in range(2) for d in range(strips_y)]
    top = strips_y - 1

    def along_to(a, b, d):
        if a == 1:
            return (1, b, d - 1) if d > 0 else (0, b, d)
        return (0, b, d + 1) if d < top else (1, b, d)

    def across_to(a, b, d):
        if a == 1:
            return (0, b, d + 1) if d < top else (1, 1 - b, d)
        return (1, b, d - 1) if d > 0 else (0, 1 - b, d)

    along_pairs = [(joint(*v), joint(*along_to(*v))) for v in everyone]
    across_pairs = [(joint(*v), joint(*across_to(*v))) for v in everyone]
    flip_pairs = [(0, 2), (1, 3), (2, 0), (3, 1)]
    core_pairs = [(0, 1), (1, 0), (2, 3), (3, 2)]
    forth = [(i, (i + 1) % slabs) for i in range(slabs)]
    back = [(b, a) for a, b in forth]

    both_pairs = [(s * 4 + a, (s - 1) % slabs * 4 + b) for s in range(slabs) for a, b in core_pairs]
    diagonal_pairs = [(0, 3), (1, 2), (2, 1), (3, 0)]

    own, flip, along, across, home = call(
        pack_kernel,
        [shape(TILE + HALF, count, LANES)] * 2 + [shape(HALF, count, LANES)] * 2 + [shape(2, rows, LANES)],
        "hhhhhh",
        [pltpu.SMEM((2,), F32), pltpu.SMEM((2,), F32), pltpu.VMEM(materials.shape, jnp.int32), pltpu.VMEM((6, rows, LANES), F32), pltpu.SemaphoreType.DMA((9,))],
    )(*(pltpu.with_memory_space_constraint(x, pltpu.HBM) for x in (conductivity, sink_rate, start, forcing, cond_field, materials)))
    other = lax.ppermute(flip, "sx", flip_pairs)
    along = lax.ppermute(along, ("sx", "sy"), along_pairs)
    across = lax.ppermute(across, ("sx", "sy"), across_pairs)

    next_own = lax.ppermute(own[:BLOCK], "slab", back)
    other, along, across, next_own = lax.optimization_barrier((other, along, across, next_own))
    mine, send, rest = call(
        window_kernel,
        [shape(2, WIDE, count, LANES)] * 2 + [shape(2 * BLOCK, count, LANES)],
        "vvvv",
        [pltpu.VMEM((BLOCK, count, LANES), F32), pltpu.SemaphoreType.DMA((2,))],

    )(own, other, along, across)
    theirs = lax.ppermute(send, "sx", core_pairs)

    their_own = lax.ppermute(next_own, "sx", core_pairs)
    next_rest = lax.ppermute(rest, "slab", back)
    their_rest = lax.ppermute(rest, ("slab", "sx"), both_pairs)

    theirs, their_own = lax.optimization_barrier((theirs, their_own))

    whole = shape(BLOCK, lines, LANES)
    flat = shape(lines, LANES)
    strip = shape(2, BLOCK, count, LANES)
    buffer = pltpu.VMEM((BLOCK, lines + 2 * BLOCK, LANES), F32)
    plain = pltpu.VMEM((BLOCK, lines, LANES), F32)
    scaled = [plain] * 5 + [pltpu.VMEM((2, lines, LANES), F32)]
    states, ends, south, north, east, west, base, sink = call(
        functools.partial(forward_kernel, 4 * strips_y),
        [shape(STEPS * BLOCK, lines, LANES), strip, whole, whole, whole, flat, whole, flat],
        "vv",
        [buffer, plain, buffer, plain, plain, buffer, buffer] + scaled,
        flops=20_000_000,
    )(mine, theirs)
    previous = lax.ppermute(ends, "slab", forth)
    (adjoint,) = call(adjoint_kernel, [strip], "v" * 11, [buffer, buffer, plain] + scaled, flops=10_000_000)(
        states, next_own, next_rest, their_own, their_rest, south, north, east, west, base, sink
    )

    low_lanes = lax.broadcasted_iota(jnp.int32, (BLOCK, count, LANES), 2) < STRIP

    def strip_for(chip, owner):
        a = lax.dynamic_index_in_dim(adjoint, owner, 0, keepdims=False)
        e = lax.dynamic_index_in_dim(previous, owner, 0, keepdims=False)
        return jnp.where(low_lanes == (chip == 0), a, e)

    keep, core, flip, both = (strip_for(*to) for to in ((y, c), (y, 1 - c), (1 - y, c), (1 - y, 1 - c)))
    flip = lax.ppermute(flip, "sx", flip_pairs)
    both = lax.ppermute(both, "sx", diagonal_pairs)
    core = lax.ppermute(core, "sx", core_pairs)
    defect, gradient = call(
        join_kernel,
        [shape(rows, 2 * LANES)] * 2,
        "vvvvv",
        [pltpu.VMEM((2, 2, rows, LANES), F32), pltpu.SemaphoreType.DMA((2, 2))],
        out_specs=[HBM] * 2,
    )(home, keep, core, flip, both)
    return (defect[None], gradient[None])


def solution(mesh):
    placed = (P("slab", "sx", "sy"), P("slab", "sx", "sy"), P("sx", "sy"), P("sx", "sy"), P(), P())
    return jax.shard_map(
        functools.partial(per_device, mesh.shape["slab"], mesh.shape["sy"]),
        mesh=mesh,
        in_specs=placed,
        out_specs=(P("slab", "sx", "sy"), P("slab", "sx", "sy")),
        check_vma=False,
    )
```

```python
import functools

import jax
import jax.numpy as jnp
from jax import lax
from jax.experimental import pallas as pl
from jax.experimental.pallas import tpu as pltpu
from jax.sharding import PartitionSpec as P

BLOCK = 8
STEPS = 3
NEWTON = 2
JACOBI = 4
LANES = 128
HALO = 32
STRIP = LANES - 2 * HALO
CHUNK = 16

time_step = 2.0
half_step = 0.5 * time_step

VMEM = pl.BlockSpec(memory_space=pltpu.VMEM)
SMEM = pl.BlockSpec(memory_space=pltpu.SMEM)
HBM = pl.BlockSpec(memory_space=pltpu.HBM)
F32 = jnp.float32


def roll(x, shift):
    return pltpu.roll(x, shift % LANES, axis=x.ndim - 1)


def lanes_of(x):
    return lax.broadcasted_iota(jnp.int32, x.shape, x.ndim - 1)


def position():
    sx = lax.axis_index("sx")
    return sx // 2, lax.rem(sx, 2), 4 * lax.axis_index("sy") + sx


def pick(test, a, b):
    return jnp.where(test, a, b)


TILE = 3 * BLOCK + 1
HALF = BLOCK + 1
WIDE = 4 * BLOCK + 1


def first_pack(s, f, k):
    at = lanes_of(s)
    far = jnp.where(at == 96, roll(s, 64), roll(k, 65))
    return jnp.where(at < 32, s, jnp.where(at < 64, roll(f, 32), jnp.where(at < 96, roll(k, 64), far)))


def last_pack(s, f, k):
    at = lanes_of(s)
    far = jnp.where(at == 96, roll(s, 1), roll(k, 2))
    return jnp.where(at < 32, roll(s, 32), jnp.where(at < 64, roll(f, 64), jnp.where(at < 96, roll(k, 96), far)))


def pack_kernel(scales, rates, start, source, cond, elements, own, flip, along, across, home, conductivity, sinks, materials, split, done):
    y, _, _ = position()
    copies = [pltpu.make_async_copy(scales, conductivity, done.at[7]), pltpu.make_async_copy(rates, sinks, done.at[8])]
    copies.append(pltpu.make_async_copy(elements, materials, done.at[0]))
    for a, ref in enumerate((start, source, cond)):
        for half in range(2):
            part = ref.at[:, pl.ds(half * LANES, LANES)]
            copies.append(pltpu.make_async_copy(part, split.at[2 * a + half], done.at[1 + 2 * a + half]))
    for copy in copies:
        copy.start()
    count, cells = materials.shape
    width = start.shape[1]
    column = lax.broadcasted_iota(jnp.int32, (cells, width), 1)
    cell = lax.broadcasted_iota(jnp.int32, (cells, width), 0)
    spread = jnp.where(column // BLOCK == cell, 1.0, 0.0).astype(F32)
    for copy in copies[:3]:
        copy.wait()
    material = jnp.dot(materials[...].astype(F32), spread, preferred_element_type=F32)
    is_gob = material > 0.5
    factor = jnp.where(is_gob, conductivity[1], conductivity[0])
    sink = time_step * jnp.where(is_gob, sinks[1], sinks[0])
    m0, m1 = sink[:, :LANES], sink[:, LANES:]
    lower = y == 0

    def place(p, tiles, packs):
        (first0, last0, first1, last1) = packs
        if tiles is not None:
            for a, (x0, x1) in enumerate(tiles):
                own[a * BLOCK + p] = pick(lower, x0, x1)
                flip[a * BLOCK + p] = pick(lower, x1, x0)
        own[TILE + p] = pick(lower, first1, last0)
        flip[TILE + p] = pick(lower, last0, first1)
        along[p] = pick(lower, last1, first0)
        across[p] = pick(lower, first0, last1)

    for copy in copies[3:]:
        copy.wait()
    home[0] = split[0]
    home[1] = split[1]
    for p in range(BLOCK):
        rows = pl.ds(p, count, stride=BLOCK)
        s0, s1, f0, f1, k0, k1 = (split[a, rows, :] for a in range(6))
        k0, k1 = k0 * factor[:, :LANES], k1 * factor[:, LANES:]
        packs = (first_pack(s0, f0, k0), last_pack(s0, f0, k0), first_pack(s1, f1, k1), last_pack(s1, f1, k1))
        place(p, ((s0, s1), (f0, f1), (k0, k1)), packs)
    own[3 * BLOCK] = pick(lower, m0, m1)
    flip[3 * BLOCK] = pick(lower, m1, m0)
    place(BLOCK, None, (m0, roll(m0, 32), m1, roll(m1, 32)))


def window_kernel(own, other, along, across, next_own, mine, theirs, rest, beside, done):
    y, c, _ = position()
    lower, even = y == 0, c == 0
    at = lax.broadcasted_iota(jnp.int32, own.shape[1:], 1)

    def put(slot, index, left, right):
        mine[slot, index] = pick(even, left, right)
        theirs[slot, index] = pick(even, right, left)

    for p in range(BLOCK):
        west0, east0 = pick(lower, along[p], own[TILE + p]), pick(lower, own[TILE + p], along[p])
        west1, east1 = pick(lower, across[p], other[TILE + p]), pick(lower, other[TILE + p], across[p])
        high = jnp.where(at < 96, roll(west1, 64), roll(east1, 96))
        beside[p] = jnp.where(at < 32, west0, jnp.where(at < 64, roll(east0, 32), high))
    parts = ((other.at[pl.ds(0, BLOCK)], 0), (beside, 1))
    copies = [pltpu.make_async_copy(part, rest.at[pl.ds(i * BLOCK, BLOCK)], done.at[i]) for part, i in parts]
    for copy in copies:
        copy.start()
    for p in range(BLOCK):
        theirs[p // 4, WIDE + p % 4] = next_own[p]
    for slot, (tile, outer) in enumerate(((own, along), (other, across))):
        for p in range(BLOCK + 1):
            inner, far = tile[TILE + p], outer[p]
            west, east = pick(lower, far, inner), pick(lower, inner, far)
            if p == BLOCK:
                m = tile[3 * BLOCK]
                put(slot, 4 * BLOCK, jnp.where(at < 32, west, roll(m, 32)), jnp.where(at >= 96, roll(east, 96), roll(m, 96)))
                continue
            s, f, k = tile[p], tile[BLOCK + p], tile[2 * BLOCK + p]
            for a, x in enumerate((s, f, k)):
                left = jnp.where(at < 32, roll(west, -32 * a), roll(x, 32))
                right = jnp.where(at >= 96, roll(east, 96 - 32 * a), roll(x, 96))
                put(slot, a * BLOCK + p, left, right)
            left = jnp.where(at < 2, roll(west, 32), jnp.where(at == 127, roll(s, 31), roll(k, 30)))
            right = jnp.where(at == 0, roll(s, 97), jnp.where(at == 1, roll(k, 98), jnp.where(at == 127, roll(east, 31), roll(east, 29))))
            put(slot, 3 * BLOCK + p, left, right)
    for copy in copies:
        copy.wait()


def chunks(lines):
    for first in range(0, lines, CHUNK):
        yield first


def shifted(ref, p, first, by):
    return ref[p, pl.ds(BLOCK + first + by, CHUNK), :]


def padded(ref, p, first):
    return ref[p, pl.ds(BLOCK + first, CHUNK), :]


def put_padded(ref, p, first, value):
    ref[p, pl.ds(BLOCK + first, CHUNK), :] = value


def clear_ends(ref, lines):
    zero = jnp.zeros((BLOCK, LANES), F32)
    for p in (0, BLOCK - 1):
        ref[p, 0:BLOCK, :] = zero
        ref[p, BLOCK + lines : 2 * BLOCK + lines, :] = zero


def factor_and_solve(first, diagonal, right, south, north, east, west, scaled, answer):
    at = pl.ds(first, CHUNK)
    keep_right, keep_south, keep_north, keep_lower, keep_upper, keep_ends = scaled
    values = []
    ratio = None
    value = None
    edge = None
    for p in range(BLOCK):
        pivot = diagonal(p)
        if p:
            pivot = pivot - edge * ratio
        inverse = 1.0 / pivot
        scaled_right = right(p) * inverse
        keep_right[p, at, :] = scaled_right
        keep_south[p, at, :] = south[p, at, :] * inverse
        keep_north[p, at, :] = north[p, at, :] * inverse
        if p == 0:
            keep_ends[0, at, :] = west[at, :] * inverse
            value = scaled_right
        else:
            lower = edge * inverse
            keep_lower[p, at, :] = lower
            value = scaled_right + lower * value
        edge = east[p, at, :]
        ratio = edge * inverse
        if p < BLOCK - 1:
            keep_upper[p, at, :] = ratio
        else:
            keep_ends[1, at, :] = ratio
        values.append(value)
    back_substitute(first, values, keep_upper, lambda p, z: put_padded(answer, p, first, z))


def back_substitute(first, values, upper, store):
    at = pl.ds(first, CHUNK)
    z = values[BLOCK - 1]
    store(BLOCK - 1, z)
    for p in range(BLOCK - 2, -1, -1):
        z = values[p] + upper[p, at, :] * z
        store(p, z)


def sweep(lines, scaled, old, store):
    keep_right, keep_south, keep_north, keep_lower, keep_upper, keep_ends = scaled
    for first in chunks(lines):
        at = pl.ds(first, CHUNK)
        values = []
        for p in range(BLOCK):
            z = padded(old, p, first)
            value = keep_right[p, at, :] + keep_south[p, at, :] * roll(z, 1) + keep_north[p, at, :] * roll(z, -1)
            if p == 0:
                value = value + keep_ends[0, at, :] * shifted(old, BLOCK - 1, first, -1)
            if p == BLOCK - 1:
                value = value + keep_ends[1, at, :] * shifted(old, 0, first, 1)
            if p:
                value = value + keep_lower[p, at, :] * values[-1]
            values.append(value)
        back_substitute(first, values, keep_upper, functools.partial(store, first))


def put_into(ref):
    return lambda first, p, z: put_padded(ref, p, first, z)


def forward_kernel(strips, mine, theirs, states, ends, south, north, east, west, base, sink, level, forcing, kappa, edge, previous, old, new, *scaled):
    y, c, strip = position()
    lines = base.shape[1]
    count = mine.shape[2]
    for ref in (level, kappa, old, new):
        clear_ends(ref, lines)
    lane = lax.broadcasted_iota(jnp.int32, (count, LANES), 1)
    column = strip * STRIP - HALO + lane
    inside = (column >= 0) & (column < strips * STRIP)

    for ref, core in ((mine, c), (theirs, 1 - c)):
        for slot in range(2):
            chip = y if slot == 0 else 1 - y
            first = pl.multiple_of((2 * chip + core) * count, BLOCK)
            for p in range(BLOCK):
                level[p, pl.ds(BLOCK + first, count), :] = ref[slot, p]
                forcing[p, pl.ds(first, count), :] = time_step * ref[slot, BLOCK + p]
                kappa[p, pl.ds(BLOCK + first, count), :] = jnp.where(inside, ref[slot, 2 * BLOCK + p], 0.0)
                edge[p, pl.ds(first, count), :] = ref[slot, 3 * BLOCK + p]
            sink[pl.ds(first, count), :] = ref[slot, 4 * BLOCK]

    lane = lax.broadcasted_iota(jnp.int32, (CHUNK, LANES), 1)
    column = strip * STRIP - HALO + lane
    is_first = lane == 0
    is_last = lane == LANES - 1
    has_south = column != 0
    has_north = column != strips * STRIP - 1
    before = strip * STRIP - HALO > 0
    after = strip * STRIP - HALO + LANES < strips * STRIP

    for first in chunks(lines):
        at = pl.ds(first, CHUNK)
        k = [padded(kappa, p, first) for p in range(BLOCK)]
        wests = [half_step * (k[0] + shifted(kappa, BLOCK - 1, first, -1))]
        wests += [half_step * (k[p] + k[p - 1]) for p in range(1, BLOCK)]
        wests += [half_step * (k[BLOCK - 1] + shifted(kappa, 0, first, 1))]
        west[at, :] = wests[0]
        for p in range(BLOCK):
            side = edge[p, at, :]
            below = jnp.where(is_first, jnp.where(before, roll(side, -1), 0.0), roll(k[p], 1))
            above = jnp.where(is_last, jnp.where(after, roll(side, 1), 0.0), roll(k[p], -1))
            s = half_step * (k[p] + below)
            n = half_step * (k[p] + above)
            base[p, at, :] = 1.0 + (wests[p] + wests[p + 1] + s + n)
            south[p, at, :] = jnp.where(has_south, s, 0.0)
            north[p, at, :] = jnp.where(has_north, n, 0.0)
            east[p, at, :] = wests[p + 1]

    def newton(from_previous, store):
        for first in chunks(lines):
            at = pl.ds(first, CHUNK)
            sink_here = sink[at, :]
            tangents = {}
            currents = {}

            def state(p):
                if p not in currents:
                    currents[p] = padded(level, p, first)
                    tangents[p] = jnp.tanh(currents[p])
                return currents[p], tangents[p]

            def diagonal(p):
                _, tangent = state(p)
                return base[p, at, :] + sink_here * (1.0 - tangent * tangent)

            def right(p):
                current, tangent = state(p)
                below, above = roll(current, 1), roll(current, -1)
                if from_previous:
                    side = edge[p, at, :]
                    below, above = jnp.where(is_first, side, below), jnp.where(is_last, side, above)
                behind = padded(level, p - 1, first) if p else shifted(level, BLOCK - 1, first, -1)
                ahead = padded(level, p + 1, first) if p < BLOCK - 1 else shifted(level, 0, first, 1)
                behind_edge = east[p - 1, at, :] if p else west[at, :]
                pulled = (south[p, at, :] * below + north[p, at, :] * above + behind_edge * behind + east[p, at, :] * ahead)
                if from_previous:
                    held = current + forcing[p, at, :]
                    previous[p, at, :] = held
                else:
                    held = previous[p, at, :]
                return held - base[p, at, :] * current + pulled - sink_here * tangent

            factor_and_solve(first, diagonal, right, south, north, east, west, scaled, old)
        sweep(lines, scaled, old, put_into(new))
        sweep(lines, scaled, new, put_into(old))
        sweep(lines, scaled, old, store)

    def step(number, carry):
        def store(keep, first, p, z):
            value = padded(level, p, first) + z
            put_padded(level, p, first, value)
            if keep:
                states[number * BLOCK + p, pl.ds(first, CHUNK), :] = value

        for turn in range(NEWTON):
            newton(turn == 0, functools.partial(store, turn == NEWTON - 1))
        return carry

    lax.fori_loop(0, STEPS, step, 0)
    pack_strip(lambda p, first: level[p, pl.ds(BLOCK + first, count), :], ends, True)


def pack_strip(read, out, swapped=False):
    count = out.shape[2]
    at = lax.broadcasted_iota(jnp.int32, (count, LANES), 1)
    for core in range(2):
        for p in range(BLOCK):
            low, high = read(p, core * count), read(p, (2 + core) * count)
            if swapped:
                low, high = high, low
            out[core, p] = jnp.where(at < STRIP, roll(low, -HALO), roll(high, HALO))


def adjoint_kernel(states, own, rest, theirs, their_rest, south, north, east, west, base, sink, out, old, new, given, *scaled):
    y, c, _ = position()
    lines = base.shape[1]
    count = own.shape[1]
    for ref in (old, new):
        clear_ends(ref, lines)
    lane = lax.broadcasted_iota(jnp.int32, (count, LANES), 1)
    even = c == 0
    turn = jnp.where(even, HALO, LANES - HALO)
    edge = jnp.where(even, lane, lane - (LANES - HALO))
    from_side = (edge >= 0) & (edge < HALO)
    for others, core in ((rest, c), (their_rest, 1 - c)):
        for slot in range(2):
            chip = y if slot == 0 else 1 - y
            at = pl.ds(pl.multiple_of((2 * chip + core) * count, BLOCK), count)
            side_turn = jnp.where(even, (LANES - 2 * HALO * slot) % LANES, (2 * LANES - 2 * HALO - 2 * HALO * slot) % LANES)
            for p in range(BLOCK):
                tile = pltpu.roll(others[p] if slot else own[p] if others is rest else theirs[p // 4, WIDE + p % 4], turn, axis=1)
                side = pltpu.roll(others[BLOCK + p], side_turn, axis=1)
                start = jnp.where(from_side, side, tile)
                given[p, at, :] = states[(STEPS - 1) * BLOCK + p, at, :] - start

    def step(number, carry):
        level = STEPS - 1 - number
        for first in chunks(lines):
            at = pl.ds(first, CHUNK)
            sink_here = sink[at, :]

            def diagonal(p):
                tangent = jnp.tanh(states[level * BLOCK + p, at, :])
                return base[p, at, :] + sink_here * (1.0 - tangent * tangent)

            def right(p):
                return given[p, at, :]

            factor_and_solve(first, diagonal, right, south, north, east, west, scaled, old)
        sweep(lines, scaled, old, put_into(new))
        sweep(lines, scaled, new, put_into(old))

        def store(first, p, z):
            given[p, pl.ds(first, CHUNK), :] = z

        sweep(lines, scaled, old, store)
        return carry

    lax.fori_loop(0, STEPS, step, 0)
    pack_strip(lambda p, first: given[p, pl.ds(first, count), :], out)


def join_kernel(home, keep, core, flip, both, defect, gradient, built, done):
    y, c, _ = position()
    count = keep.shape[1]
    at = lax.broadcasted_iota(jnp.int32, (count, LANES), 1)
    copies = []
    for chip in range(2):
        here = y == chip
        for p in range(BLOCK):
            one, two = pick(here, keep[p], flip[p]), pick(here, core[p], both[p])
            even, odd = pick(c == 0, one, two), pick(c == 0, two, one)
            low, high = jnp.where(at < STRIP, even, roll(odd, STRIP)), jnp.where(at < STRIP, roll(even, STRIP), odd)
            rows = pl.ds(p, count, stride=BLOCK)
            missed = pick(y == 0, high, low) - home[chip, rows, :]
            built[0, chip, rows, :] = missed
            built[1, chip, rows, :] = pick(y == 0, low, high) - missed
        for a, out in enumerate((defect, gradient)):
            copies.append(pltpu.make_async_copy(built.at[a, chip], out.at[:, pl.ds(chip * LANES, LANES)], done.at[a, chip]))
            copies[-1].start()
    for copy in copies:
        copy.wait()


def per_device(slabs, strips_y, start_states, source, cond_field, materials, conductivity, sink_rate):
    sx = lax.axis_index("sx")
    y, c = sx // 2, sx % 2
    start, forcing = start_states[0], source[0]
    rows = start.shape[0]
    count = rows // BLOCK
    lines = 4 * count
    shape = lambda *dims: jax.ShapeDtypeStruct(dims, F32)
    params = pltpu.CompilerParams(vmem_limit_bytes=16 * 1024 * 1024)

    def call(body, outs, ins, scratch=(), flops=0, out_specs=None):
        specs = [{"s": SMEM, "v": VMEM, "h": HBM}[kind] for kind in ins]
        cost = pl.CostEstimate(flops=flops, bytes_accessed=1 << 20, transcendentals=0)
        out_specs = out_specs or [VMEM] * len(outs)
        return pl.pallas_call(body, out_shape=outs, in_specs=specs, out_specs=out_specs, scratch_shapes=list(scratch), compiler_params=params, cost_estimate=cost)

    def joint(y_, c_, z_):
        return (2 * y_ + c_) * strips_y + z_

    everyone = [(a, b, d) for a in range(2) for b in range(2) for d in range(strips_y)]
    top = strips_y - 1

    def along_to(a, b, d):
        if a == 1:
            return (1, b, d - 1) if d > 0 else (0, b, d)
        return (0, b, d + 1) if d < top else (1, b, d)

    def across_to(a, b, d):
        if a == 1:
            return (0, b, d + 1) if d < top else (1, 1 - b, d)
        return (1, b, d - 1) if d > 0 else (0, 1 - b, d)

    along_pairs = [(joint(*v), joint(*along_to(*v))) for v in everyone]
    across_pairs = [(joint(*v), joint(*across_to(*v))) for v in everyone]
    flip_pairs = [(0, 2), (1, 3), (2, 0), (3, 1)]
    core_pairs = [(0, 1), (1, 0), (2, 3), (3, 2)]
    forth = [(i, (i + 1) % slabs) for i in range(slabs)]
    back = [(b, a) for a, b in forth]

    both_pairs = [(s * 4 + a, (s - 1) % slabs * 4 + b) for s in range(slabs) for a, b in core_pairs]
    diagonal_pairs = [(0, 3), (1, 2), (2, 1), (3, 0)]

    own, flip, along, across, home = call(
        pack_kernel,
        [shape(TILE + HALF, count, LANES)] * 2 + [shape(HALF, count, LANES)] * 2 + [shape(2, rows, LANES)],
        "hhhhhh",
        [pltpu.SMEM((2,), F32), pltpu.SMEM((2,), F32), pltpu.VMEM(materials.shape, jnp.int32), pltpu.VMEM((6, rows, LANES), F32), pltpu.SemaphoreType.DMA((9,))],
    )(*(pltpu.with_memory_space_constraint(x, pltpu.HBM) for x in (conductivity, sink_rate, start, forcing, cond_field, materials)))
    other = lax.ppermute(flip, "sx", flip_pairs)
    along = lax.ppermute(along, ("sx", "sy"), along_pairs)
    across = lax.ppermute(across, ("sx", "sy"), across_pairs)

    next_own = lax.ppermute(own[:BLOCK], "slab", back)
    mine, send, rest = call(
        window_kernel,
        [shape(2, WIDE, count, LANES), shape(2, WIDE + 4, count, LANES), shape(2 * BLOCK, count, LANES)],
        "vvvvv",
        [pltpu.VMEM((BLOCK, count, LANES), F32), pltpu.SemaphoreType.DMA((2,))],

    )(own, other, along, across, next_own)
    theirs = lax.ppermute(send, "sx", core_pairs)

    next_rest = lax.ppermute(rest, "slab", back)
    their_rest = lax.ppermute(rest, ("slab", "sx"), both_pairs)

    whole = shape(BLOCK, lines, LANES)
    flat = shape(lines, LANES)
    strip = shape(2, BLOCK, count, LANES)
    buffer = pltpu.VMEM((BLOCK, lines + 2 * BLOCK, LANES), F32)
    plain = pltpu.VMEM((BLOCK, lines, LANES), F32)
    scaled = [plain] * 5 + [pltpu.VMEM((2, lines, LANES), F32)]
    states, ends, south, north, east, west, base, sink = call(
        functools.partial(forward_kernel, 4 * strips_y),
        [shape(STEPS * BLOCK, lines, LANES), strip, whole, whole, whole, flat, whole, flat],
        "vv",
        [buffer, plain, buffer, plain, plain, buffer, buffer] + scaled,
        flops=20_000_000,
    )(mine, theirs)
    previous = lax.ppermute(ends, "slab", forth)
    (adjoint,) = call(adjoint_kernel, [strip], "v" * 11, [buffer, buffer, plain] + scaled, flops=10_000_000)(
        states, next_own, next_rest, theirs, their_rest, south, north, east, west, base, sink
    )

    low_lanes = lax.broadcasted_iota(jnp.int32, (BLOCK, count, LANES), 2) < STRIP

    def strip_for(chip, owner):
        a = lax.dynamic_index_in_dim(adjoint, owner, 0, keepdims=False)
        e = lax.dynamic_index_in_dim(previous, owner, 0, keepdims=False)
        return jnp.where(low_lanes == (chip == 0), a, e)

    keep, core, flip, both = (strip_for(*to) for to in ((y, c), (y, 1 - c), (1 - y, c), (1 - y, 1 - c)))
    flip = lax.ppermute(flip, "sx", flip_pairs)
    both = lax.ppermute(both, "sx", diagonal_pairs)
    core = lax.ppermute(core, "sx", core_pairs)
    defect, gradient = call(
        join_kernel,
        [shape(rows, 2 * LANES)] * 2,
        "vvvvv",
        [pltpu.VMEM((2, 2, rows, LANES), F32), pltpu.SemaphoreType.DMA((2, 2))],
        out_specs=[HBM] * 2,
    )(home, keep, core, flip, both)
    return (defect[None], gradient[None])


def solution(mesh):
    placed = (P("slab", "sx", "sy"), P("slab", "sx", "sy"), P("sx", "sy"), P("sx", "sy"), P(), P())
    return jax.shard_map(
        functools.partial(per_device, mesh.shape["slab"], mesh.shape["sy"]),
        mesh=mesh,
        in_specs=placed,
        out_specs=(P("slab", "sx", "sy"), P("slab", "sx", "sy")),
        check_vma=False,
    )
```

```python
import functools

import jax
import jax.numpy as jnp
from jax import lax
from jax.experimental import pallas as pl
from jax.experimental.pallas import tpu as pltpu
from jax.sharding import PartitionSpec as P

BLOCK = 8
STEPS = 3
NEWTON = 2
JACOBI = 4
LANES = 128
HALO = 32
STRIP = LANES - 2 * HALO
CHUNK = 16

time_step = 2.0
half_step = 0.5 * time_step

VMEM = pl.BlockSpec(memory_space=pltpu.VMEM)
SMEM = pl.BlockSpec(memory_space=pltpu.SMEM)
HBM = pl.BlockSpec(memory_space=pltpu.HBM)
F32 = jnp.float32


def roll(x, shift):
    return pltpu.roll(x, shift % LANES, axis=x.ndim - 1)


def lanes_of(x):
    return lax.broadcasted_iota(jnp.int32, x.shape, x.ndim - 1)


def position():
    sx = lax.axis_index("sx")
    return sx // 2, lax.rem(sx, 2), 4 * lax.axis_index("sy") + sx


def pick(test, a, b):
    return jnp.where(test, a, b)


TILE = 3 * BLOCK + 1
HALF = BLOCK + 1
WIDE = 4 * BLOCK + 1


def first_pack(s, f, k):
    at = lanes_of(s)
    far = jnp.where(at == 96, roll(s, 64), roll(k, 65))
    return jnp.where(at < 32, s, jnp.where(at < 64, roll(f, 32), jnp.where(at < 96, roll(k, 64), far)))


def last_pack(s, f, k):
    at = lanes_of(s)
    far = jnp.where(at == 96, roll(s, 1), roll(k, 2))
    return jnp.where(at < 32, roll(s, 32), jnp.where(at < 64, roll(f, 64), jnp.where(at < 96, roll(k, 96), far)))


def pack_kernel(scales, rates, start, source, cond, elements, own, flip, along, across, home, conductivity, sinks, materials, split, done):
    y, _, _ = position()
    copies = [pltpu.make_async_copy(scales, conductivity, done.at[7]), pltpu.make_async_copy(rates, sinks, done.at[8])]
    copies.append(pltpu.make_async_copy(elements, materials, done.at[0]))
    for a, ref in enumerate((start, source, cond)):
        for half in range(2):
            part = ref.at[:, pl.ds(half * LANES, LANES)]
            copies.append(pltpu.make_async_copy(part, split.at[2 * a + half], done.at[1 + 2 * a + half]))
    for copy in copies:
        copy.start()
    count, cells = materials.shape
    width = start.shape[1]
    column = lax.broadcasted_iota(jnp.int32, (cells, width), 1)
    cell = lax.broadcasted_iota(jnp.int32, (cells, width), 0)
    spread = jnp.where(column // BLOCK == cell, 1.0, 0.0).astype(F32)
    for copy in copies[:3]:
        copy.wait()
    material = jnp.dot(materials[...].astype(F32), spread, preferred_element_type=F32)
    is_gob = material > 0.5
    factor = jnp.where(is_gob, conductivity[1], conductivity[0])
    sink = time_step * jnp.where(is_gob, sinks[1], sinks[0])
    m0, m1 = sink[:, :LANES], sink[:, LANES:]
    lower = y == 0

    def place(p, tiles, packs):
        (first0, last0, first1, last1) = packs
        if tiles is not None:
            for a, (x0, x1) in enumerate(tiles):
                own[a * BLOCK + p] = pick(lower, x0, x1)
                flip[a * BLOCK + p] = pick(lower, x1, x0)
        own[TILE + p] = pick(lower, first1, last0)
        flip[TILE + p] = pick(lower, last0, first1)
        along[p] = pick(lower, last1, first0)
        across[p] = pick(lower, first0, last1)

    for copy in copies[3:]:
        copy.wait()
    home[0] = split[0]
    home[1] = split[1]
    for p in range(BLOCK):
        rows = pl.ds(p, count, stride=BLOCK)
        s0, s1, f0, f1, k0, k1 = (split[a, rows, :] for a in range(6))
        k0, k1 = k0 * factor[:, :LANES], k1 * factor[:, LANES:]
        packs = (first_pack(s0, f0, k0), last_pack(s0, f0, k0), first_pack(s1, f1, k1), last_pack(s1, f1, k1))
        place(p, ((s0, s1), (f0, f1), (k0, k1)), packs)
    own[3 * BLOCK] = pick(lower, m0, m1)
    flip[3 * BLOCK] = pick(lower, m1, m0)
    place(BLOCK, None, (m0, roll(m0, 32), m1, roll(m1, 32)))


def window_kernel(own, other, along, across, next_own, mine, theirs, rest):
    y, c, _ = position()
    lower, even = y == 0, c == 0
    at = lax.broadcasted_iota(jnp.int32, own.shape[1:], 1)

    def put(slot, index, left, right):
        mine[slot, index] = pick(even, left, right)
        theirs[slot, index] = pick(even, right, left)

    for p in range(BLOCK):
        west0, east0 = pick(lower, along[p], own[TILE + p]), pick(lower, own[TILE + p], along[p])
        west1, east1 = pick(lower, across[p], other[TILE + p]), pick(lower, other[TILE + p], across[p])
        high = jnp.where(at < 96, roll(west1, 64), roll(east1, 96))
        rest[p] = other[p]
        rest[BLOCK + p] = jnp.where(at < 32, west0, jnp.where(at < 64, roll(east0, 32), high))
    for p in range(BLOCK):
        theirs[p // 4, WIDE + p % 4] = next_own[p]
    for slot, (tile, outer) in enumerate(((own, along), (other, across))):
        for p in range(BLOCK + 1):
            inner, far = tile[TILE + p], outer[p]
            west, east = pick(lower, far, inner), pick(lower, inner, far)
            if p == BLOCK:
                m = tile[3 * BLOCK]
                put(slot, 4 * BLOCK, jnp.where(at < 32, west, roll(m, 32)), jnp.where(at >= 96, roll(east, 96), roll(m, 96)))
                continue
            s, f, k = tile[p], tile[BLOCK + p], tile[2 * BLOCK + p]
            for a, x in enumerate((s, f, k)):
                left = jnp.where(at < 32, roll(west, -32 * a), roll(x, 32))
                right = jnp.where(at >= 96, roll(east, 96 - 32 * a), roll(x, 96))
                put(slot, a * BLOCK + p, left, right)
            left = jnp.where(at < 2, roll(west, 32), jnp.where(at == 127, roll(s, 31), roll(k, 30)))
            right = jnp.where(at == 0, roll(s, 97), jnp.where(at == 1, roll(k, 98), jnp.where(at == 127, roll(east, 31), roll(east, 29))))
            put(slot, 3 * BLOCK + p, left, right)


def chunks(lines):
    for first in range(0, lines, CHUNK):
        yield first


def shifted(ref, p, first, by):
    return ref[p, pl.ds(BLOCK + first + by, CHUNK), :]


def padded(ref, p, first):
    return ref[p, pl.ds(BLOCK + first, CHUNK), :]


def put_padded(ref, p, first, value):
    ref[p, pl.ds(BLOCK + first, CHUNK), :] = value


def clear_ends(ref, lines):
    zero = jnp.zeros((BLOCK, LANES), F32)
    for p in (0, BLOCK - 1):
        ref[p, 0:BLOCK, :] = zero
        ref[p, BLOCK + lines : 2 * BLOCK + lines, :] = zero


def factor_and_solve(first, diagonal, right, south, north, east, west, scaled, answer):
    at = pl.ds(first, CHUNK)
    keep_right, keep_south, keep_north, keep_lower, keep_upper, keep_ends = scaled
    values = []
    ratio = None
    value = None
    edge = None
    for p in range(BLOCK):
        pivot = diagonal(p)
        if p:
            pivot = pivot - edge * ratio
        inverse = 1.0 / pivot
        scaled_right = right(p) * inverse
        keep_right[p, at, :] = scaled_right
        keep_south[p, at, :] = south[p, at, :] * inverse
        keep_north[p, at, :] = north[p, at, :] * inverse
        if p == 0:
            keep_ends[0, at, :] = west[at, :] * inverse
            value = scaled_right
        else:
            lower = edge * inverse
            keep_lower[p, at, :] = lower
            value = scaled_right + lower * value
        edge = east[p, at, :]
        ratio = edge * inverse
        if p < BLOCK - 1:
            keep_upper[p, at, :] = ratio
        else:
            keep_ends[1, at, :] = ratio
        values.append(value)
    back_substitute(first, values, keep_upper, lambda p, z: put_padded(answer, p, first, z))


def back_substitute(first, values, upper, store):
    at = pl.ds(first, CHUNK)
    z = values[BLOCK - 1]
    store(BLOCK - 1, z)
    for p in range(BLOCK - 2, -1, -1):
        z = values[p] + upper[p, at, :] * z
        store(p, z)


def sweep(lines, scaled, old, store):
    keep_right, keep_south, keep_north, keep_lower, keep_upper, keep_ends = scaled
    for first in chunks(lines):
        at = pl.ds(first, CHUNK)
        values = []
        for p in range(BLOCK):
            z = padded(old, p, first)
            value = keep_right[p, at, :] + keep_south[p, at, :] * roll(z, 1) + keep_north[p, at, :] * roll(z, -1)
            if p == 0:
                value = value + keep_ends[0, at, :] * shifted(old, BLOCK - 1, first, -1)
            if p == BLOCK - 1:
                value = value + keep_ends[1, at, :] * shifted(old, 0, first, 1)
            if p:
                value = value + keep_lower[p, at, :] * values[-1]
            values.append(value)
        back_substitute(first, values, keep_upper, functools.partial(store, first))


def put_into(ref):
    return lambda first, p, z: put_padded(ref, p, first, z)


def forward_kernel(strips, mine, theirs, states, ends, south, north, east, west, base, sink, level, forcing, kappa, edge, previous, old, new, *scaled):
    y, c, strip = position()
    lines = base.shape[1]
    count = mine.shape[2]
    for ref in (level, kappa, old, new):
        clear_ends(ref, lines)
    lane = lax.broadcasted_iota(jnp.int32, (count, LANES), 1)
    column = strip * STRIP - HALO + lane
    inside = (column >= 0) & (column < strips * STRIP)

    for ref, core in ((mine, c), (theirs, 1 - c)):
        for slot in range(2):
            chip = y if slot == 0 else 1 - y
            first = pl.multiple_of((2 * chip + core) * count, BLOCK)
            for p in range(BLOCK):
                level[p, pl.ds(BLOCK + first, count), :] = ref[slot, p]
                forcing[p, pl.ds(first, count), :] = time_step * ref[slot, BLOCK + p]
                kappa[p, pl.ds(BLOCK + first, count), :] = jnp.where(inside, ref[slot, 2 * BLOCK + p], 0.0)
                edge[p, pl.ds(first, count), :] = ref[slot, 3 * BLOCK + p]
            sink[pl.ds(first, count), :] = ref[slot, 4 * BLOCK]

    lane = lax.broadcasted_iota(jnp.int32, (CHUNK, LANES), 1)
    column = strip * STRIP - HALO + lane
    is_first = lane == 0
    is_last = lane == LANES - 1
    has_south = column != 0
    has_north = column != strips * STRIP - 1
    before = strip * STRIP - HALO > 0
    after = strip * STRIP - HALO + LANES < strips * STRIP

    for first in chunks(lines):
        at = pl.ds(first, CHUNK)
        k = [padded(kappa, p, first) for p in range(BLOCK)]
        wests = [half_step * (k[0] + shifted(kappa, BLOCK - 1, first, -1))]
        wests += [half_step * (k[p] + k[p - 1]) for p in range(1, BLOCK)]
        wests += [half_step * (k[BLOCK - 1] + shifted(kappa, 0, first, 1))]
        west[at, :] = wests[0]
        for p in range(BLOCK):
            side = edge[p, at, :]
            below = jnp.where(is_first, jnp.where(before, roll(side, -1), 0.0), roll(k[p], 1))
            above = jnp.where(is_last, jnp.where(after, roll(side, 1), 0.0), roll(k[p], -1))
            s = half_step * (k[p] + below)
            n = half_step * (k[p] + above)
            base[p, at, :] = 1.0 + (wests[p] + wests[p + 1] + s + n)
            south[p, at, :] = jnp.where(has_south, s, 0.0)
            north[p, at, :] = jnp.where(has_north, n, 0.0)
            east[p, at, :] = wests[p + 1]

    def newton(from_previous, store):
        for first in chunks(lines):
            at = pl.ds(first, CHUNK)
            sink_here = sink[at, :]
            tangents = {}
            currents = {}

            def state(p):
                if p not in currents:
                    currents[p] = padded(level, p, first)
                    tangents[p] = jnp.tanh(currents[p])
                return currents[p], tangents[p]

            def diagonal(p):
                _, tangent = state(p)
                return base[p, at, :] + sink_here * (1.0 - tangent * tangent)

            def right(p):
                current, tangent = state(p)
                below, above = roll(current, 1), roll(current, -1)
                if from_previous:
                    side = edge[p, at, :]
                    below, above = jnp.where(is_first, side, below), jnp.where(is_last, side, above)
                behind = padded(level, p - 1, first) if p else shifted(level, BLOCK - 1, first, -1)
                ahead = padded(level, p + 1, first) if p < BLOCK - 1 else shifted(level, 0, first, 1)
                behind_edge = east[p - 1, at, :] if p else west[at, :]
                pulled = (south[p, at, :] * below + north[p, at, :] * above + behind_edge * behind + east[p, at, :] * ahead)
                if from_previous:
                    held = current + forcing[p, at, :]
                    previous[p, at, :] = held
                else:
                    held = previous[p, at, :]
                return held - base[p, at, :] * current + pulled - sink_here * tangent

            factor_and_solve(first, diagonal, right, south, north, east, west, scaled, old)
        sweep(lines, scaled, old, put_into(new))
        sweep(lines, scaled, new, put_into(old))
        sweep(lines, scaled, old, store)

    def step(number, carry):
        def store(keep, first, p, z):
            value = padded(level, p, first) + z
            put_padded(level, p, first, value)
            if keep:
                states[number * BLOCK + p, pl.ds(first, CHUNK), :] = value

        for turn in range(NEWTON):
            newton(turn == 0, functools.partial(store, turn == NEWTON - 1))
        return carry

    lax.fori_loop(0, STEPS, step, 0)
    pack_strip(lambda p, first: level[p, pl.ds(BLOCK + first, count), :], ends, True)


def pack_strip(read, out, swapped=False):
    count = out.shape[2]
    at = lax.broadcasted_iota(jnp.int32, (count, LANES), 1)
    for core in range(2):
        for p in range(BLOCK):
            low, high = read(p, core * count), read(p, (2 + core) * count)
            if swapped:
                low, high = high, low
            out[core, p] = jnp.where(at < STRIP, roll(low, -HALO), roll(high, HALO))


def adjoint_kernel(states, own, rest, theirs, their_rest, south, north, east, west, base, sink, out, old, new, given, *scaled):
    y, c, _ = position()
    lines = base.shape[1]
    count = own.shape[1]
    for ref in (old, new):
        clear_ends(ref, lines)
    lane = lax.broadcasted_iota(jnp.int32, (count, LANES), 1)
    even = c == 0
    turn = jnp.where(even, HALO, LANES - HALO)
    edge = jnp.where(even, lane, lane - (LANES - HALO))
    from_side = (edge >= 0) & (edge < HALO)
    for others, core in ((rest, c), (their_rest, 1 - c)):
        for slot in range(2):
            chip = y if slot == 0 else 1 - y
            at = pl.ds(pl.multiple_of((2 * chip + core) * count, BLOCK), count)
            side_turn = jnp.where(even, (LANES - 2 * HALO * slot) % LANES, (2 * LANES - 2 * HALO - 2 * HALO * slot) % LANES)
            for p in range(BLOCK):
                tile = pltpu.roll(others[p] if slot else own[p] if others is rest else theirs[p // 4, WIDE + p % 4], turn, axis=1)
                side = pltpu.roll(others[BLOCK + p], side_turn, axis=1)
                start = jnp.where(from_side, side, tile)
                given[p, at, :] = states[(STEPS - 1) * BLOCK + p, at, :] - start

    def step(number, carry):
        level = STEPS - 1 - number
        for first in chunks(lines):
            at = pl.ds(first, CHUNK)
            sink_here = sink[at, :]

            def diagonal(p):
                tangent = jnp.tanh(states[level * BLOCK + p, at, :])
                return base[p, at, :] + sink_here * (1.0 - tangent * tangent)

            def right(p):
                return given[p, at, :]

            factor_and_solve(first, diagonal, right, south, north, east, west, scaled, old)
        sweep(lines, scaled, old, put_into(new))
        sweep(lines, scaled, new, put_into(old))

        def store(first, p, z):
            given[p, pl.ds(first, CHUNK), :] = z

        sweep(lines, scaled, old, store)
        return carry

    lax.fori_loop(0, STEPS, step, 0)
    pack_strip(lambda p, first: given[p, pl.ds(first, count), :], out)


def join_kernel(home, keep, core, flip, both, defect, gradient, built, done):
    y, c, _ = position()
    count = keep.shape[1]
    at = lax.broadcasted_iota(jnp.int32, (count, LANES), 1)
    copies = []
    for chip in range(2):
        here = y == chip
        for p in range(BLOCK):
            one, two = pick(here, keep[p], flip[p]), pick(here, core[p], both[p])
            even, odd = pick(c == 0, one, two), pick(c == 0, two, one)
            low, high = jnp.where(at < STRIP, even, roll(odd, STRIP)), jnp.where(at < STRIP, roll(even, STRIP), odd)
            rows = pl.ds(p, count, stride=BLOCK)
            missed = pick(y == 0, high, low) - home[chip, rows, :]
            built[0, chip, rows, :] = missed
            built[1, chip, rows, :] = pick(y == 0, low, high) - missed
        for a, out in enumerate((defect, gradient)):
            copies.append(pltpu.make_async_copy(built.at[a, chip], out.at[:, pl.ds(chip * LANES, LANES)], done.at[a, chip]))
            copies[-1].start()
    for copy in copies:
        copy.wait()


def per_device(slabs, strips_y, start_states, source, cond_field, materials, conductivity, sink_rate):
    sx = lax.axis_index("sx")
    y, c = sx // 2, sx % 2
    start, forcing = start_states[0], source[0]
    rows = start.shape[0]
    count = rows // BLOCK
    lines = 4 * count
    shape = lambda *dims: jax.ShapeDtypeStruct(dims, F32)
    params = pltpu.CompilerParams(vmem_limit_bytes=16 * 1024 * 1024)

    def call(body, outs, ins, scratch=(), flops=0, out_specs=None):
        specs = [{"s": SMEM, "v": VMEM, "h": HBM}[kind] for kind in ins]
        cost = pl.CostEstimate(flops=flops, bytes_accessed=1 << 20, transcendentals=0)
        out_specs = out_specs or [VMEM] * len(outs)
        return pl.pallas_call(body, out_shape=outs, in_specs=specs, out_specs=out_specs, scratch_shapes=list(scratch), compiler_params=params, cost_estimate=cost)

    def joint(y_, c_, z_):
        return (2 * y_ + c_) * strips_y + z_

    everyone = [(a, b, d) for a in range(2) for b in range(2) for d in range(strips_y)]
    top = strips_y - 1

    def along_to(a, b, d):
        if a == 1:
            return (1, b, d - 1) if d > 0 else (0, b, d)
        return (0, b, d + 1) if d < top else (1, b, d)

    def across_to(a, b, d):
        if a == 1:
            return (0, b, d + 1) if d < top else (1, 1 - b, d)
        return (1, b, d - 1) if d > 0 else (0, 1 - b, d)

    along_pairs = [(joint(*v), joint(*along_to(*v))) for v in everyone]
    across_pairs = [(joint(*v), joint(*across_to(*v))) for v in everyone]
    flip_pairs = [(0, 2), (1, 3), (2, 0), (3, 1)]
    core_pairs = [(0, 1), (1, 0), (2, 3), (3, 2)]
    forth = [(i, (i + 1) % slabs) for i in range(slabs)]
    back = [(b, a) for a, b in forth]

    both_pairs = [(s * 4 + a, (s - 1) % slabs * 4 + b) for s in range(slabs) for a, b in core_pairs]
    diagonal_pairs = [(0, 3), (1, 2), (2, 1), (3, 0)]

    own, flip, along, across, home = call(
        pack_kernel,
        [shape(TILE + HALF, count, LANES)] * 2 + [shape(HALF, count, LANES)] * 2 + [shape(2, rows, LANES)],
        "hhhhhh",
        [pltpu.SMEM((2,), F32), pltpu.SMEM((2,), F32), pltpu.VMEM(materials.shape, jnp.int32), pltpu.VMEM((6, rows, LANES), F32), pltpu.SemaphoreType.DMA((9,))],
    )(*(pltpu.with_memory_space_constraint(x, pltpu.HBM) for x in (conductivity, sink_rate, start, forcing, cond_field, materials)))
    other = lax.ppermute(flip, "sx", flip_pairs)
    along = lax.ppermute(along, ("sx", "sy"), along_pairs)
    across = lax.ppermute(across, ("sx", "sy"), across_pairs)

    next_own = lax.ppermute(own[:BLOCK], "slab", back)
    mine, send, rest = call(
        window_kernel,
        [shape(2, WIDE, count, LANES), shape(2, WIDE + 4, count, LANES), shape(2 * BLOCK, count, LANES)],
        "vvvvv",

    )(own, other, along, across, next_own)
    theirs = lax.ppermute(send, "sx", core_pairs)

    next_rest = lax.ppermute(rest, "slab", back)
    their_rest = lax.ppermute(rest, ("slab", "sx"), both_pairs)

    whole = shape(BLOCK, lines, LANES)
    flat = shape(lines, LANES)
    strip = shape(2, BLOCK, count, LANES)
    buffer = pltpu.VMEM((BLOCK, lines + 2 * BLOCK, LANES), F32)
    plain = pltpu.VMEM((BLOCK, lines, LANES), F32)
    scaled = [plain] * 5 + [pltpu.VMEM((2, lines, LANES), F32)]
    states, ends, south, north, east, west, base, sink = call(
        functools.partial(forward_kernel, 4 * strips_y),
        [shape(STEPS * BLOCK, lines, LANES), strip, whole, whole, whole, flat, whole, flat],
        "vv",
        [buffer, plain, buffer, plain, plain, buffer, buffer] + scaled,
        flops=20_000_000,
    )(mine, theirs)
    previous = lax.ppermute(ends, "slab", forth)
    (adjoint,) = call(adjoint_kernel, [strip], "v" * 11, [buffer, buffer, plain] + scaled, flops=10_000_000)(
        states, next_own, next_rest, theirs, their_rest, south, north, east, west, base, sink
    )

    low_lanes = lax.broadcasted_iota(jnp.int32, (BLOCK, count, LANES), 2) < STRIP

    def strip_for(chip, owner):
        a = lax.dynamic_index_in_dim(adjoint, owner, 0, keepdims=False)
        e = lax.dynamic_index_in_dim(previous, owner, 0, keepdims=False)
        return jnp.where(low_lanes == (chip == 0), a, e)

    keep, core, flip, both = (strip_for(*to) for to in ((y, c), (y, 1 - c), (1 - y, c), (1 - y, 1 - c)))
    flip = lax.ppermute(flip, "sx", flip_pairs)
    both = lax.ppermute(both, "sx", diagonal_pairs)
    core = lax.ppermute(core, "sx", core_pairs)
    defect, gradient = call(
        join_kernel,
        [shape(rows, 2 * LANES)] * 2,
        "vvvvv",
        [pltpu.VMEM((2, 2, rows, LANES), F32), pltpu.SemaphoreType.DMA((2, 2))],
        out_specs=[HBM] * 2,
    )(home, keep, core, flip, both)
    return (defect[None], gradient[None])


def solution(mesh):
    placed = (P("slab", "sx", "sy"), P("slab", "sx", "sy"), P("sx", "sy"), P("sx", "sy"), P(), P())
    return jax.shard_map(
        functools.partial(per_device, mesh.shape["slab"], mesh.shape["sy"]),
        mesh=mesh,
        in_specs=placed,
        out_specs=(P("slab", "sx", "sy"), P("slab", "sx", "sy")),
        check_vma=False,
    )
```
